32 devices in a mesh: lat: 4 (over x, core), lon: 8 (over z, y).
Axes of the slice: x: 2, y: 2, z: 4, core: 2. Of those that a mesh axis runs over, the one named last changes fastest.
Arguments:
- tokens: bfloat16 [1, 48, 96, 512], P(None, 'lat', 'lon'), may hold values from -8 to 8
- gain_first: float32 [512], replicated, may hold values from 0.1 to 1.9
- qkv_first: bfloat16 [512, 1536], replicated, may hold values from -16 to 16
- proj_first: bfloat16 [512, 512], replicated, may hold values from -0.25 to 0.25
- bias_first: float32 [4, 16, 529], P('lat'), may hold values from -6 to 6
- gain_second: float32 [512], replicated, may hold values from 0.1 to 1.9
- qkv_second: bfloat16 [512, 1536], replicated, may hold values from -16 to 16
- proj_second: bfloat16 [512, 512], replicated, may hold values from -0.25 to 0.25
- bias_second: float32 [4, 16, 529], P('lat'), may hold values from -6 to 6
Outputs:
- mixed: bfloat16 [1, 48, 96, 512], P(None, 'lat', 'lon')
The draws below stay inside these ranges and needn't reach their ends.
All inputs are finite; a program needn't handle non-finite values.
Results may differ from the reference program's by a relative error of at most 0.012.
The reference program's roundings to bfloat16 on the way count: a program that leaves them out, or rounds other values in their place, can miss the bound.
Values may be sent and summed in bfloat16 or wider, within the bound.
No kernel may reach another device: no remote copies, remote signals or barrier semaphores. Data moves between devices by JAX's collectives and lax.ppermute only.
A program may use at most 64 MiB of HBM per device.

```python
import jax
import jax.numpy as jnp
from jax import lax

D = 512
HEADS = 16
LEV = 1
WH = 12
WW = 12
NREL = 529
NLW = 4
NY = 48
NX = 96


def draw_tokens(key, part):
    own = jax.random.fold_in(key, 3)
    base = jnp.clip(jax.random.normal(own, (LEV, NY, NX, D), jnp.float32), -6.0, 6.0)
    return base.astype(jnp.bfloat16)


def projection_law(key):
    scale = D ** (-0.5)
    w_query = jnp.clip(jax.random.normal(jax.random.fold_in(key, 1), (D, D), jnp.float32), -5.0, 5.0) * scale
    w_value = jnp.clip(jax.random.normal(jax.random.fold_in(key, 2), (D, D), jnp.float32), -5.0, 5.0) * scale
    w_keys = jnp.clip(jax.random.normal(jax.random.fold_in(key, 3), (D, D), jnp.float32), -5.0, 5.0) * scale
    joined = jnp.concatenate([w_query, w_keys, w_value], axis=1)
    return jnp.clip(joined, -16.0, 16.0).astype(jnp.bfloat16)


def draw_qkv_first(key, part):
    return projection_law(jax.random.fold_in(key, 11))


def draw_qkv_second(key, part):
    return projection_law(jax.random.fold_in(key, 12))


def block_scale(own_key, shape, pieces, low, top_value):
    level, own = 1.0, jax.random.fold_in(own_key, 6)
    for axis_at, shards_of in pieces:
        draws = jnp.exp(jax.random.uniform(jax.random.fold_in(own, axis_at), (shards_of,), jnp.float32, low / len(pieces), top_value / len(pieces)))
        level = level * jnp.repeat(draws, shape[axis_at] // shards_of).reshape([-1 if axis == axis_at else 1 for axis in range(len(shape))])
    return level


def scatter_about(key, shape, deviation, bound, pieces=(), held_as=jnp.bfloat16):
    entries = deviation * jax.random.normal(key, shape, jnp.float32)
    if pieces:
        entries = entries * block_scale(key, shape, pieces, -0.22, 0.18)
    return jnp.clip(entries, -bound, bound).astype(held_as)


def setup_inputs(seed: int = 0) -> dict:
    arg_keys = jax.random.split(jax.random.key(seed), 10)
    return {
        "tokens": draw_tokens(jax.random.fold_in(arg_keys[9], 71), 0),
        "gain_first": jnp.clip(1.0 + 0.18 * jax.random.normal(arg_keys[1], (D,), jnp.float32), 0.1, 1.9),
        "qkv_first": draw_qkv_first(jax.random.fold_in(arg_keys[9], 71), 0),
        "proj_first": scatter_about(arg_keys[3], (D, D), D ** -0.5, 0.25),
        "bias_first": scatter_about(arg_keys[4], (NLW, HEADS, NREL), 1.0, 6.0, ((0, 4),), jnp.float32),
        "gain_second": jnp.clip(1.0 + 0.18 * jax.random.normal(arg_keys[5], (D,), jnp.float32), 0.1, 1.9),
        "qkv_second": draw_qkv_second(jax.random.fold_in(arg_keys[9], 71), 0),
        "proj_second": scatter_about(arg_keys[7], (D, D), D ** -0.5, 0.25),
        "bias_second": scatter_about(arg_keys[8], (NLW, HEADS, NREL), 1.0, 6.0, ((0, 4),), jnp.float32),
    }


def offsets():
    count = LEV * WH * WW
    index = jnp.arange(count, dtype=jnp.int32)
    level = index // (WH * WW)
    row = index // WW % WH
    column = index % WW
    first = level[:, None] - level[None, :] + LEV - 1
    second = row[:, None] - row[None, :] + WH - 1
    third = column[:, None] - column[None, :] + WW - 1
    return ((first * (2 * WH - 1) + second) * (2 * WW - 1) + third).astype(jnp.int32)

def to_windows(tile):
    levels, rows, cols, width = tile.shape
    shaped = tile.reshape(levels, rows, cols // WW, WW, width)
    return shaped.transpose(2, 0, 1, 3, 4).reshape(cols // WW, levels * rows * WW, width)

def from_windows(wins, cols):
    width = wins.shape[-1]
    shaped = wins.reshape(cols // WW, LEV, WH, WW, width)
    return shaped.transpose(1, 2, 0, 3, 4).reshape(LEV, WH, cols, width)

def norm_rows(values, gain):
    data = values.astype(jnp.float32)
    mean = lax.optimization_barrier(jnp.mean(data, axis=-1, keepdims=True))
    centred = data - mean
    var = lax.optimization_barrier(jnp.mean(centred * centred, axis=-1, keepdims=True))
    return (centred * lax.rsqrt(var + 1e-05) * gain).astype(jnp.bfloat16)

def attend(normed, wqkv, wproj, bias, allowed):
    count = normed.shape[0]
    size = normed.shape[1]
    width = normed.shape[2]
    head_dim = width // HEADS
    mixed = jnp.dot(normed.reshape(-1, width), wqkv, preferred_element_type=jnp.float32)
    mixed = mixed.reshape(count, size, 3, HEADS, head_dim)
    query = mixed[:, :, 0]
    keys = mixed[:, :, 1]
    values = mixed[:, :, 2].astype(jnp.bfloat16)
    scores = jnp.einsum('wqhd,wkhd->whqk', query, keys, precision=lax.Precision.HIGHEST)
    scores = scores * head_dim ** (-0.5) + bias[None]
    scores = jnp.where(allowed[None, None], scores, -1e+30)
    top = lax.optimization_barrier(jnp.max(scores, axis=-1, keepdims=True))
    expo = jnp.exp(scores - top)
    weights = (expo / lax.optimization_barrier(jnp.sum(expo, axis=-1, keepdims=True))).astype(jnp.bfloat16)
    heads_out = jnp.einsum('whqk,wkhd->wqhd', weights.astype(jnp.float32), values.astype(jnp.float32))
    heads_out = heads_out.reshape(count * size, width).astype(jnp.bfloat16)
    return jnp.dot(heads_out, wproj, preferred_element_type=jnp.float32).reshape(count, size, width)

def section(inputs, gain, wqkv, wproj, table, shifted):
    rel = offsets()
    count = LEV * WH * WW
    index = jnp.arange(count, dtype=jnp.int32)
    lower = index // WW % WH >= WH // 2
    total_rows = inputs.shape[1]
    total_cols = inputs.shape[2]
    nrows = total_rows // WH
    if shifted:
        inputs = jnp.roll(inputs, (-(WH // 2), -(WW // 2)), axis=(1, 2))

    def one_row(i):
        rows = lax.dynamic_slice_in_dim(inputs, i * WH, WH, 1)
        wins = to_windows(rows)
        normed = norm_rows(wins, gain)
        bias = jnp.take(lax.dynamic_index_in_dim(table, i, 0, keepdims=False), rel, axis=1)
        if shifted:
            group = jnp.logical_and(lower, i == nrows - 1)
        else:
            group = jnp.zeros((count,), dtype=bool)
        allowed = group[:, None] == group[None, :]
        result = wins.astype(jnp.float32) + attend(normed, wqkv, wproj, bias, allowed)
        return from_windows(result.astype(jnp.bfloat16), total_cols)
    blocks = lax.map(one_row, jnp.arange(nrows, dtype=jnp.int32))
    result = blocks.transpose(1, 0, 2, 3, 4).reshape(LEV, total_rows, total_cols, inputs.shape[3])
    if shifted:
        result = jnp.roll(result, (WH // 2, WW // 2), axis=(1, 2))
    return result

def reference(tokens, gain_first, qkv_first, proj_first, bias_first, gain_second, qkv_second, proj_second, bias_second):
    first = section(tokens, gain_first, qkv_first, proj_first, bias_first, False)
    return section(first, gain_second, qkv_second, proj_second, bias_second, True)
```

```python
import functools

import jax
import jax.numpy as jnp
from jax import lax
from jax.experimental import pallas as pl
from jax.experimental.pallas import tpu as pltpu
from jax.sharding import PartitionSpec as P

HEADS = 16
WH = 12
WW = 12
LANES = 128
SUB = 8
PITCH = 16
KEYS = 256
SPAN_R = 2 * WH - 1
SPAN_C = 2 * WW - 1
HALF_R = WH // 2
HALF_C = WW // 2
REST = WW - SUB
NEG = -1e30
F32 = jnp.float32
BF16 = jnp.bfloat16


def iota(shape, dim):
    return lax.broadcasted_iota(jnp.int32, shape, dim)


def bias_strips(table, tab, strips):
    heads = table.shape[1]
    count = table.shape[2]
    tab[...] = jnp.zeros_like(tab)
    tab[:, :count] = table[0]
    lane = iota((SUB, LANES), 1)
    row = iota((SUB, LANES), 0)
    plans = []
    for tile in range(2):
        for k in range(3):
            u = lane + k * LANES
            j = u // PITCH
            key_col = u % PITCH
            if tile == 0:
                col = row
                step = j
            else:
                second = row >= REST
                col = SUB + jnp.where(second, row - REST, row)
                step = jnp.where(second, j - 1, j)
            good = (key_col < WW) & (step >= 0) & (step < SPAN_R)
            index = (SPAN_R - 1 - step) * SPAN_C + col - key_col + WW - 1
            index = jnp.where(good, index, 0)
            top = (SPAN_R - 1 - max(8 * k - tile, 0)) * SPAN_C + SPAN_C - 1
            low = max(SPAN_R - 1 - (8 * k + 7), 0) * SPAN_C
            sources = range(low // LANES, top // LANES + 1)
            plans.append((tile, k, index % LANES, index // LANES, good, sources))
    for h in range(heads):
        rows = {}
        for tile, k, inner, outer, good, sources in plans:
            value = jnp.full((SUB, LANES), NEG, F32)
            for s in sources:
                if s not in rows:
                    rows[s] = jnp.broadcast_to(tab[h : h + 1, s * LANES : (s + 1) * LANES], (SUB, LANES))
                taken = jnp.take_along_axis(rows[s], inner, axis=1)
                value = jnp.where(good & (outer == s), taken, value)
            strips[h, tile, :, k * LANES : (k + 1) * LANES] = value


def head_bias(strips, h):
    turned = {}
    lane = iota((SUB, LANES), 1)

    def turn(tile, k, by):
        key = (tile, k, by)
        if key not in turned:
            part = strips[h, tile, :, k * LANES : (k + 1) * LANES]
            turned[key] = pltpu.roll(part, LANES - by, 1) if by else part
        return turned[key]

    def window(tile, start):
        first, by = divmod(start, LANES)
        out = []
        for k in (first, first + 1):
            left = turn(tile, k % 3, by)
            out.append(jnp.where(lane < LANES - by, left, turn(tile, (k + 1) % 3, by)) if by else left)
        return out

    tiles = [window(0, PITCH * (WH - 1 - r)) for r in range(WH)]
    tiles += [window(1, PITCH * (WH - 1 - r)) for r in range(0, WH, 2)]
    return tiles


def masks(polar):
    lane = iota((SUB, LANES), 1)
    row = iota((SUB, LANES), 0)
    out = []
    for t in range(WH + WH // 2):
        if t < WH:
            r = jnp.full((SUB, LANES), t, jnp.int32)
        else:
            r = 2 * (t - WH) + jnp.where(row >= REST, 1, 0)
        pair = []
        for k in range(2):
            key_row = (lane + k * LANES) // PITCH
            bad = key_row >= WH
            if polar is not None:
                bad = bad | (((r >= HALF_R) != (key_row >= HALF_R)) & polar)
            pair.append(jnp.where(bad, NEG, 0.0).astype(F32))
        out.append(pair)
    return out


def compact(value):
    width = value.shape[-1]
    tiles = value.reshape(WH, 2, SUB, width)
    row = iota((SUB, width), 0)
    parts = [tiles[r, 0] for r in range(WH)]
    for r in range(0, WH, 2):
        parts.append(jnp.where(row < REST, tiles[r, 1], pltpu.roll(tiles[r + 1, 1], REST, 0)))
    return jnp.concatenate(parts, axis=0)


def attend(xs, ys, table, gain, wqkv, wproj, tab, strips, probs, polar):
    width = xs.shape[-1]
    heads = HEADS
    head_dim = width // heads
    group = LANES // head_dim
    tokens = WH * WW
    x = xs[...].reshape(WH * PITCH, width)
    mean = jnp.mean(x, axis=-1, keepdims=True)
    centred = x - mean
    var = jnp.mean(centred * centred, axis=-1, keepdims=True)
    normed = (centred * lax.rsqrt(var + 1e-05) * gain[...]).astype(BF16)
    bias_strips(table, tab, strips)
    mixed = jnp.dot(normed, wqkv[...], preferred_element_type=F32)
    query = compact(mixed[:, :width]) * head_dim ** (-0.5)
    keys = mixed[:, width : 2 * width]
    pad = jnp.zeros((KEYS - WH * PITCH, width), BF16)
    values = jnp.concatenate([mixed[:, 2 * width :].astype(BF16), pad], axis=0)
    q_hi = query.astype(BF16)
    q_lo = (query - q_hi.astype(F32)).astype(BF16)
    k_hi = keys.astype(BF16)
    k_lo = (keys - k_hi.astype(F32)).astype(BF16)
    k_hi = jnp.concatenate([k_hi, pad], axis=0)
    k_lo = jnp.concatenate([k_lo, pad], axis=0)
    lane = iota((1, LANES), 1)
    extra = masks(polar)
    outs = []
    for g in range(heads // group):
        part = slice(g * LANES, (g + 1) * LANES)
        left = jnp.concatenate([q_hi[:, part], q_lo[:, part], q_hi[:, part]], axis=1)
        rights = []
        for i in range(group):
            own = (lane // head_dim == i).astype(BF16)
            kh = k_hi[:, part] * own
            kl = k_lo[:, part] * own
            right = jnp.concatenate([kh, kh, kl], axis=1)
            scores = lax.dot_general(left, right, (((1,), (1,)), ((), ())), preferred_element_type=F32)
            tiles = head_bias(strips, g * group + i)
            for t in range(0, len(tiles), 2):
                pair = []
                for u in (t, t + 1):
                    rows = slice(u * SUB, (u + 1) * SUB)
                    s0 = scores[rows, :LANES] + tiles[u][0]
                    s1 = scores[rows, LANES:] + tiles[u][1] + extra[u][1]
                    if polar is not None:
                        s0 = s0 + extra[u][0]
                    top = jnp.max(jnp.maximum(s0, s1), axis=-1, keepdims=True)
                    e0 = jnp.exp(s0 - top)
                    e1 = jnp.exp(s1 - top)
                    total = jnp.sum(e0 + e1, axis=-1, keepdims=True)
                    inverse = 1.0 / total
                    pair.append(jnp.concatenate([e0 * inverse, e1 * inverse], axis=1))
                probs[t * SUB : (t + 2) * SUB, i * KEYS : (i + 1) * KEYS] = jnp.concatenate(pair, axis=0).astype(BF16)
            rights.append(values[:, part] * own)
        outs.append(jnp.dot(probs[...], jnp.concatenate(rights, axis=0), preferred_element_type=F32))
    heads_out = jnp.concatenate(outs, axis=1).astype(BF16)
    branch = jnp.dot(heads_out, wproj[...], preferred_element_type=F32)
    for r in range(WH):
        ys[r, :SUB, :] = xs[r, :SUB, :] + branch[r * SUB : (r + 1) * SUB]
        at = WH * SUB + r * REST
        ys[r, SUB:WW, :] = xs[r, SUB:WW, :] + branch[at : at + REST]


def quadrants(ys, outs):
    at = 0
    for r in (0, HALF_R):
        for c in (0, HALF_C):
            outs[at][...] = ys[r : r + HALF_R, c : c + HALF_C, :].astype(BF16)
            at += 1


def first_kernel(tokens, table, gain, wqkv, wproj, nw, ne, sw, se, xs, ys, tab, strips, probs):
    xs[:, WW:, :] = jnp.zeros((WH, PITCH - WW, xs.shape[-1]), F32)
    xs[:, :WW, :] = tokens[0].astype(F32)
    attend(xs, ys, table, gain, wqkv, wproj, tab, strips, probs, None)
    quadrants(ys, (nw, ne, sw, se))


def second_kernel(nw_in, ne_in, sw_in, se_in, table, gain, wqkv, wproj, nw, ne, sw, se, xs, ys, tab, strips, probs):
    polar = lax.axis_index("lat") == lax.axis_size("lat") - 1
    xs[:, WW:, :] = jnp.zeros((WH, PITCH - WW, xs.shape[-1]), F32)
    at = 0
    pieces = (nw_in, ne_in, sw_in, se_in)
    for r in (0, HALF_R):
        for c in (0, HALF_C):
            xs[r : r + HALF_R, c : c + HALF_C, :] = pieces[at][...].astype(F32)
            at += 1
    attend(xs, ys, table, gain, wqkv, wproj, tab, strips, probs, polar)
    quadrants(ys, (nw, ne, sw, se))


def block(kernel, pieces, table, gain, wqkv, wproj):
    width = wproj.shape[0]
    heads, count = table.shape[1:]
    lanes = -(-count // LANES) * LANES
    piece = jax.ShapeDtypeStruct((HALF_R, HALF_C, width), BF16)
    args = (*pieces, table, gain.reshape(1, width), wqkv, wproj)
    vmem = pl.BlockSpec(memory_space=pltpu.VMEM)
    return pl.pallas_call(
        kernel,
        out_shape=(piece,) * 4,
        in_specs=[vmem] * len(args),
        out_specs=(vmem,) * 4,
        scratch_shapes=[
            pltpu.VMEM((WH, PITCH, width), F32),
            pltpu.VMEM((WH, PITCH, width), F32),
            pltpu.VMEM((heads, lanes), F32),
            pltpu.VMEM((heads, 2, SUB, 3 * LANES), F32),
            pltpu.VMEM((WH * WW, LANES // (width // heads) * KEYS), BF16),
        ],
        compiler_params=pltpu.CompilerParams(vmem_limit_bytes=24 << 20),
        cost_estimate=pl.CostEstimate(flops=400_000_000, bytes_accessed=2_500_000, transcendentals=600_000),
    )(*args)


def moved(piece, lat, lon):
    rows, cols = lax.axis_size("lat"), lax.axis_size("lon")
    route = [
        (((i + lat) % rows) * cols + (j + lon) % cols, i * cols + j) for i in range(rows) for j in range(cols)
    ]
    return lax.ppermute(piece, ("lat", "lon"), route)


def shards(
    tokens,
    gain_first,
    qkv_first,
    proj_first,
    bias_first,
    gain_second,
    qkv_second,
    proj_second,
    bias_second,
):
    nw, ne, sw, se = block(first_kernel, (tokens,), bias_first, gain_first, qkv_first, proj_first)
    window = (se, moved(sw, 0, 1), moved(ne, 1, 0), moved(nw, 1, 1))
    nw, ne, sw, se = block(second_kernel, window, bias_second, gain_second, qkv_second, proj_second)
    west, north, corner = moved(ne, 0, -1), moved(sw, -1, 0), moved(se, -1, -1)
    upper = jnp.concatenate([corner, north], axis=1)
    lower = jnp.concatenate([west, nw], axis=1)
    return jnp.concatenate([upper, lower], axis=0)[None]


def solution(mesh):
    placed = (
        P(None, "lat", "lon", None),
        P(),
        P(),
        P(),
        P("lat", None, None),
        P(),
        P(),
        P(),
        P("lat", None, None),
    )
    return jax.shard_map(
        shards, mesh=mesh, in_specs=placed, out_specs=P(None, "lat", "lon", None), check_vma=False
    )
```

```python
import functools

import jax
import jax.numpy as jnp
from jax import lax
from jax.experimental import pallas as pl
from jax.experimental.pallas import tpu as pltpu
from jax.sharding import PartitionSpec as P

HEADS = 16
WH = 12
WW = 12
LANES = 128
SUB = 8
PITCH = 16
SPAN_C = 2 * WW - 1
HALF_R = WH // 2
HALF_C = WW // 2
REST = WW - SUB
NEG = -1e30
F32 = jnp.float32
BF16 = jnp.bfloat16


def iota(shape, dim):
    return lax.broadcasted_iota(jnp.int32, shape, dim)


def bias_strips(table, tab, strips):
    heads = table.shape[1]
    count = table.shape[2]
    tab[...] = jnp.zeros_like(tab)
    tab[:, :count] = table[0]
    lane = iota((SUB, LANES), 1)
    row = iota((SUB, LANES), 0)
    plans = []
    for tile in range(2):
        for k in range(3):
            u = lane + k * LANES
            step = u // PITCH
            if tile == 0:
                col = row
            else:
                second = row >= REST
                col = SUB + jnp.where(second, row - REST, row)
                step = jnp.where(second, step - 1, step)
            index = step * SPAN_C + u % PITCH - col + WW - 1
            index = jnp.clip(index, 0, count - 1)
            low = max(8 * k - tile, 0) * SPAN_C
            top = min((8 * k + 7) * SPAN_C + PITCH + WW - 2, count - 1)
            sources = range(low // LANES, top // LANES + 1)
            plans.append((tile, k, index % LANES, index // LANES, sources))
    for h in range(heads):
        rows = {}
        for tile, k, inner, outer, sources in plans:
            value = None
            for s in sources:
                if s not in rows:
                    rows[s] = jnp.broadcast_to(tab[h : h + 1, s * LANES : (s + 1) * LANES], (SUB, LANES))
                taken = jnp.take_along_axis(rows[s], inner, axis=1)
                value = taken if value is None else jnp.where(outer == s, taken, value)
            strips[h, tile, :, k * LANES : (k + 1) * LANES] = value


def bias_tiles(strips, h):
    turned = {}
    lane = iota((SUB, LANES), 1)
    per_head = WH * PITCH

    def turn(head, tile, k, by):
        key = (head, tile, k, by)
        if key not in turned:
            part = strips[head, tile, :, k * LANES : (k + 1) * LANES]
            turned[key] = pltpu.roll(part, LANES - by, 1) if by else part
        return turned[key]

    def window(tile, start, t):
        cuts = []
        at = t * LANES
        while at < (t + 1) * LANES:
            which, query = divmod(at, per_head)
            u = start + query
            k = u // LANES
            end = min(at + (k + 1) * LANES - u, (which + 1) * per_head, (t + 1) * LANES)
            cuts.append((end - t * LANES, turn(h + which, tile, k, (u - at) % LANES)))
            at = end
        value = cuts[-1][1]
        for end, part in reversed(cuts[:-1]):
            value = jnp.where(lane < end, part, value)
        return value

    starts = [(0, PITCH * (WH - 1 - r)) for r in range(WH)]
    starts += [(1, PITCH * (WH - 1 - r)) for r in range(0, WH, 2)]
    return [[window(tile, start, t) for tile, start in starts] for t in range(2 * per_head // LANES)]


def halves(polar):
    lane = iota((SUB, LANES), 1)
    out = []
    for t in range(2 * WH * PITCH // LANES):
        query = (lane + t * LANES) % (WH * PITCH) // PITCH >= HALF_R
        out.append([jnp.where((query != lower) & polar, NEG, 0.0).astype(F32) for lower in (False, True)])
    return out


def compact(value):
    width = value.shape[-1]
    tiles = value.reshape(WH, 2, SUB, width)
    row = iota((SUB, width), 0)
    parts = [tiles[r, 0] for r in range(WH)]
    for r in range(0, WH, 2):
        parts.append(jnp.where(row < REST, tiles[r, 1], pltpu.roll(tiles[r + 1, 1], REST, 0)))
    return jnp.concatenate(parts, axis=0)


def split(value):
    high = value.astype(BF16)
    return high, (value - high.astype(F32)).astype(BF16)


def soft(scores, bias, mask, probs, at):
    count = len(bias)
    tiles = []
    for u in range(count):
        s = scores[u * SUB : (u + 1) * SUB] + bias[u]
        if mask is not None:
            lower = u >= HALF_R if u < WH else 2 * (u - WH) >= HALF_R
            s = s + mask[int(lower)]
        tiles.append(s)
    top = functools.reduce(jnp.maximum, tiles)
    top = jnp.max(top, axis=0, keepdims=True)
    tiles = [jnp.exp(s - top) for s in tiles]
    total = functools.reduce(jnp.add, tiles)
    inverse = 1.0 / jnp.sum(total, axis=0, keepdims=True)
    for u in range(0, count, 2):
        pair = jnp.concatenate([tiles[u] * inverse, tiles[u + 1] * inverse], axis=0)
        probs[u * SUB : (u + 2) * SUB, at : at + LANES] = pair.astype(BF16)


def attend(xs, ys, gain, weights, strips, probs, polar):
    width = xs.shape[-1]
    head_dim = width // HEADS
    group = LANES // head_dim
    per_head = WH * PITCH
    x = xs[...].reshape(per_head, width)
    mean = jnp.mean(x, axis=-1, keepdims=True)
    centred = x - mean
    var = jnp.mean(centred * centred, axis=-1, keepdims=True)
    normed = (centred * lax.rsqrt(var + 1e-05) * gain[...]).astype(BF16)
    wqkv = weights(0)
    mixed = jnp.dot(normed, wqkv[...], preferred_element_type=F32)
    q_hi, q_lo = split(mixed[:, :width] * head_dim ** (-0.5))
    k_hi, k_lo = split(compact(mixed[:, width : 2 * width]))
    values = compact(mixed[:, 2 * width :]).astype(BF16)
    lane = iota((1, LANES), 1)
    masks = None if polar is None else halves(polar)

    def product(g):
        part = slice(g * LANES, (g + 1) * LANES)
        left = jnp.concatenate([k_hi[:, part], k_hi[:, part], k_lo[:, part]], axis=1)
        rights = []
        for i in range(group):
            own = (lane // head_dim == i).astype(BF16)
            high = q_hi[:, part] * own
            rights.append(jnp.concatenate([high, q_lo[:, part] * own, high], axis=1))
        right = jnp.concatenate(rights, axis=0)
        return lax.dot_general(left, right, (((1,), (1,)), ((), ())), preferred_element_type=F32)

    outs = []
    groups = HEADS // group
    ahead = product(0)
    for g in range(groups):
        scores = ahead
        if g + 1 < groups:
            ahead = product(g + 1)
        for i in range(0, group, 2):
            bias = bias_tiles(strips, g * group + i)
            for t in range(len(bias)):
                at = i * per_head + t * LANES
                soft(scores[:, at : at + LANES], bias[t], masks and masks[t], probs.at[g], at)
        part = slice(g * LANES, (g + 1) * LANES)
        mixed_v = lax.dot_general(
            values[:, part], probs[g], (((0,), (0,)), ((), ())), preferred_element_type=F32
        )
        heads_out = []
        for i in range(group):
            rows = slice(i * head_dim, (i + 1) * head_dim)
            first, by = divmod(i * per_head, LANES)
            own = mixed_v[rows, first * LANES : (first + 2) * LANES]
            heads_out.append(pltpu.roll(own, 2 * LANES - by, 1) if by else own)
        outs.append(jnp.concatenate(heads_out, axis=0).T)
    heads_out = jnp.concatenate(outs, axis=1)[:per_head].astype(BF16)
    wproj = weights(1)
    branch = jnp.dot(heads_out, wproj[...], preferred_element_type=F32)
    ys[...] = xs[...] + branch.reshape(xs.shape)


def quadrants(ys, outs):
    at = 0
    for r in (0, HALF_R):
        for c in (0, HALF_C):
            outs[at][...] = ys[r : r + HALF_R, c : c + HALF_C, :].astype(BF16)
            at += 1


def first_kernel(tokens, table, gain, wqkv, wproj, nw, ne, sw, se, xs, ys, tab, strips, probs, *here):
    here, sems = here[:-1], here[-1]
    copies = [
        pltpu.make_async_copy(a, b, sems.at[i]) for i, (a, b) in enumerate(zip((table, tokens, gain, wqkv, wproj), here))
    ]
    for copy in copies:
        copy.start()
    xs[:, WW:, :] = jnp.zeros((WH, PITCH - WW, xs.shape[-1]), F32)
    copies[0].wait()
    bias_strips(here[0], tab, strips)
    copies[1].wait()
    xs[:, :WW, :] = here[1][0].astype(F32)
    copies[2].wait()

    def weights(i):
        copies[3 + i].wait()
        return here[3 + i]

    attend(xs, ys, here[2], weights, strips, probs, None)
    quadrants(ys, (nw, ne, sw, se))


def second_kernel(nw_in, ne_in, sw_in, se_in, table, gain, wqkv, wproj, nw, ne, sw, se, xs, ys, tab, strips, probs):
    polar = lax.axis_index("lat") == lax.axis_size("lat") - 1
    xs[:, WW:, :] = jnp.zeros((WH, PITCH - WW, xs.shape[-1]), F32)
    at = 0
    pieces = (nw_in, ne_in, sw_in, se_in)
    for r in (0, HALF_R):
        for c in (0, HALF_C):
            xs[r : r + HALF_R, c : c + HALF_C, :] = pieces[at][...].astype(F32)
            at += 1
    bias_strips(table, tab, strips)
    attend(xs, ys, gain, lambda i: (wqkv, wproj)[i], strips, probs, polar)
    quadrants(ys, (nw, ne, sw, se))


def block(kernel, pieces, table, gain, wqkv, wproj, fetch):
    width = wproj.shape[0]
    heads, count = table.shape[1:]
    lanes = -(-count // LANES) * LANES
    group = LANES * heads // width
    piece = jax.ShapeDtypeStruct((HALF_R, HALF_C, width), BF16)
    args = (*pieces, table, gain.reshape(1, width), wqkv, wproj)
    vmem = pl.BlockSpec(memory_space=pltpu.VMEM)
    scratch = [
        pltpu.VMEM((WH, PITCH, width), F32),
        pltpu.VMEM((WH, PITCH, width), F32),
        pltpu.VMEM((heads, lanes), F32),
        pltpu.VMEM((heads, 2, SUB, 3 * LANES), F32),
        pltpu.VMEM((heads // group, WH * WW, group * WH * PITCH), BF16),
    ]
    if fetch:
        order = (args[1], args[0], *args[2:])
        scratch += [pltpu.VMEM(a.shape, a.dtype) for a in order]
        scratch += [pltpu.SemaphoreType.DMA((len(order),))]
    source = pl.BlockSpec(memory_space=pltpu.HBM) if fetch else vmem
    return pl.pallas_call(
        kernel,
        out_shape=(piece,) * 4,
        in_specs=[source] * len(args),
        out_specs=(vmem,) * 4,
        scratch_shapes=scratch,
        compiler_params=pltpu.CompilerParams(vmem_limit_bytes=24 << 20),
        cost_estimate=pl.CostEstimate(flops=400_000_000, bytes_accessed=2_500_000, transcendentals=600_000),
    )(*args)


def moved(piece, lat, lon):
    rows, cols = lax.axis_size("lat"), lax.axis_size("lon")
    route = [
        (((i + lat) % rows) * cols + (j + lon) % cols, i * cols + j) for i in range(rows) for j in range(cols)
    ]
    return lax.ppermute(piece, ("lat", "lon"), route)


def shards(
    tokens,
    gain_first,
    qkv_first,
    proj_first,
    bias_first,
    gain_second,
    qkv_second,
    proj_second,
    bias_second,
):
    nw, ne, sw, se = block(first_kernel, (tokens,), bias_first, gain_first, qkv_first, proj_first, True)
    window = (se, moved(sw, 0, 1), moved(ne, 1, 0), moved(nw, 1, 1))
    nw, ne, sw, se = block(second_kernel, window, bias_second, gain_second, qkv_second, proj_second, False)
    west, north, corner = moved(ne, 0, -1), moved(sw, -1, 0), moved(se, -1, -1)
    upper = jnp.concatenate([corner, north], axis=1)
    lower = jnp.concatenate([west, nw], axis=1)
    return jnp.concatenate([upper, lower], axis=0)[None]


def solution(mesh):
    placed = (
        P(None, "lat", "lon", None),
        P(),
        P(),
        P(),
        P("lat", None, None),
        P(),
        P(),
        P(),
        P("lat", None, None),
    )
    return jax.shard_map(
        shards, mesh=mesh, in_specs=placed, out_specs=P(None, "lat", "lon", None), check_vma=False
    )
```

```python
import functools

import jax
import jax.numpy as jnp
from jax import lax
from jax.experimental import pallas as pl
from jax.experimental.pallas import tpu as pltpu
from jax.sharding import PartitionSpec as P

HEADS = 16
WH = 12
WW = 12
LANES = 128
SUB = 8
PITCH = 16
SPAN_C = 2 * WW - 1
HALF_R = WH // 2
HALF_C = WW // 2
REST = WW - SUB
NEG = -1e30
F32 = jnp.float32
BF16 = jnp.bfloat16


def iota(shape, dim):
    return lax.broadcasted_iota(jnp.int32, shape, dim)


def bias_strips(table, tab, strips):
    heads = table.shape[1]
    count = table.shape[2]
    tab[...] = jnp.zeros_like(tab)
    tab[:, :count] = table[0]
    lane = iota((SUB, LANES), 1)
    row = iota((SUB, LANES), 0)
    plans = []
    for tile in range(2):
        for k in range(3):
            u = lane + k * LANES
            step = u // PITCH
            if tile == 0:
                col = row
            else:
                second = row >= REST
                col = SUB + jnp.where(second, row - REST, row)
                step = jnp.where(second, step - 1, step)
            index = step * SPAN_C + u % PITCH - col + WW - 1
            index = jnp.clip(index, 0, count - 1)
            low = max(8 * k - tile, 0) * SPAN_C
            top = min((8 * k + 7) * SPAN_C + PITCH + WW - 2, count - 1)
            sources = range(low // LANES, top // LANES + 1)
            plans.append((tile, k, index % LANES, index // LANES, sources))
    for h in range(heads):
        rows = {}
        for tile, k, inner, outer, sources in plans:
            value = None
            for s in sources:
                if s not in rows:
                    rows[s] = jnp.broadcast_to(tab[h : h + 1, s * LANES : (s + 1) * LANES], (SUB, LANES))
                taken = jnp.take_along_axis(rows[s], inner, axis=1)
                value = taken if value is None else jnp.where(outer == s, taken, value)
            strips[h, tile, :, k * LANES : (k + 1) * LANES] = value


def bias_tiles(strips, h):
    turned = {}
    lane = iota((SUB, LANES), 1)
    per_head = WH * PITCH

    def turn(head, tile, k, by):
        key = (head, tile, k, by)
        if key not in turned:
            part = strips[head, tile, :, k * LANES : (k + 1) * LANES]
            turned[key] = pltpu.roll(part, LANES - by, 1) if by else part
        return turned[key]

    def window(tile, start, t):
        cuts = []
        at = t * LANES
        while at < (t + 1) * LANES:
            which, query = divmod(at, per_head)
            u = start + query
            k = u // LANES
            end = min(at + (k + 1) * LANES - u, (which + 1) * per_head, (t + 1) * LANES)
            cuts.append((end - t * LANES, turn(h + which, tile, k, (u - at) % LANES)))
            at = end
        value = cuts[-1][1]
        for end, part in reversed(cuts[:-1]):
            value = jnp.where(lane < end, part, value)
        return value

    starts = [(0, PITCH * (WH - 1 - r)) for r in range(WH)]
    starts += [(1, PITCH * (WH - 1 - r)) for r in range(0, WH, 2)]
    return [[window(tile, start, t) for tile, start in starts] for t in range(2 * per_head // LANES)]


def halves(polar):
    lane = iota((SUB, LANES), 1)
    out = []
    for t in range(2 * WH * PITCH // LANES):
        query = (lane + t * LANES) % (WH * PITCH) // PITCH >= HALF_R
        out.append([jnp.where((query != lower) & polar, NEG, 0.0).astype(F32) for lower in (False, True)])
    return out


def compact(value):
    width = value.shape[-1]
    tiles = value.reshape(WH, 2, SUB, width)
    row = iota((SUB, width), 0)
    parts = [tiles[r, 0] for r in range(WH)]
    for r in range(0, WH, 2):
        parts.append(jnp.where(row < REST, tiles[r, 1], pltpu.roll(tiles[r + 1, 1], REST, 0)))
    return jnp.concatenate(parts, axis=0)


def split(value):
    high = value.astype(BF16)
    return high, (value - high.astype(F32)).astype(BF16)


def soft(scores, bias, mask, probs, at):
    count = len(bias)
    tiles = []
    for u in range(count):
        s = scores[u * SUB : (u + 1) * SUB] + bias[u]
        if mask is not None:
            lower = u >= HALF_R if u < WH else 2 * (u - WH) >= HALF_R
            s = s + mask[int(lower)]
        tiles.append(s)
    top = functools.reduce(jnp.maximum, tiles)
    top = jnp.max(top, axis=0, keepdims=True)
    tiles = [jnp.exp(s - top) for s in tiles]
    total = functools.reduce(jnp.add, tiles)
    inverse = 1.0 / jnp.sum(total, axis=0, keepdims=True)
    for u in range(0, count, 2):
        pair = jnp.concatenate([tiles[u] * inverse, tiles[u + 1] * inverse], axis=0)
        probs[u * SUB : (u + 2) * SUB, at : at + LANES] = pair.astype(BF16)


def attend(xs, ys, gain, weights, strips, probs, polar):
    width = xs.shape[-1]
    head_dim = width // HEADS
    group = LANES // head_dim
    per_head = WH * PITCH
    x = xs[...].reshape(per_head, width)
    mean = jnp.mean(x, axis=-1, keepdims=True)
    centred = x - mean
    var = jnp.mean(centred * centred, axis=-1, keepdims=True)
    normed = (centred * lax.rsqrt(var + 1e-05) * gain[...]).astype(BF16)
    wqkv = weights(0)
    mixed = jnp.dot(normed, wqkv[...], preferred_element_type=F32)
    q_hi, q_lo = split(mixed[:, :width] * head_dim ** (-0.5))
    k_hi, k_lo = split(compact(mixed[:, width : 2 * width]))
    values = compact(mixed[:, 2 * width :]).astype(BF16)
    lane = iota((1, LANES), 1)
    masks = None if polar is None else halves(polar)

    def product(g):
        part = slice(g * LANES, (g + 1) * LANES)
        left = jnp.concatenate([k_hi[:, part], k_hi[:, part], k_lo[:, part]], axis=1)
        rights = []
        for i in range(group):
            own = (lane // head_dim == i).astype(BF16)
            high = q_hi[:, part] * own
            rights.append(jnp.concatenate([high, q_lo[:, part] * own, high], axis=1))
        right = jnp.concatenate(rights, axis=0)
        return lax.dot_general(left, right, (((1,), (1,)), ((), ())), preferred_element_type=F32)

    outs = []
    groups = HEADS // group
    ahead = product(0)
    for g in range(groups):
        scores = ahead
        if g + 1 < groups:
            ahead = product(g + 1)
        for i in range(0, group, 2):
            bias = bias_tiles(strips, g * group + i)
            for t in range(len(bias)):
                at = i * per_head + t * LANES
                soft(scores[:, at : at + LANES], bias[t], masks and masks[t], probs.at[g], at)
        part = slice(g * LANES, (g + 1) * LANES)
        mixed_v = lax.dot_general(
            values[:, part], probs[g], (((0,), (0,)), ((), ())), preferred_element_type=F32
        )
        heads_out = []
        for i in range(group):
            rows = slice(i * head_dim, (i + 1) * head_dim)
            first, by = divmod(i * per_head, LANES)
            own = mixed_v[rows, first * LANES : (first + 2) * LANES]
            heads_out.append(pltpu.roll(own, 2 * LANES - by, 1) if by else own)
        outs.append(jnp.concatenate(heads_out, axis=0).T)
    heads_out = jnp.concatenate(outs, axis=1)[:per_head].astype(BF16)
    wproj = weights(1)
    branch = jnp.dot(heads_out, wproj[...], preferred_element_type=F32)
    ys[...] = xs[...] + branch.reshape(xs.shape)


def quadrants(ys, outs):
    at = 0
    for r in (0, HALF_R):
        for c in (0, HALF_C):
            outs[at][...] = ys[r : r + HALF_R, c : c + HALF_C, :].astype(BF16)
            at += 1


def first_kernel(tokens, table, gain, wqkv, wproj, nw, ne, sw, se, xs, ys, tab, strips, probs, *here):
    here, sems = here[:-1], here[-1]
    copies = [
        pltpu.make_async_copy(a, b, sems.at[i]) for i, (a, b) in enumerate(zip((table, tokens, gain, wqkv, wproj), here))
    ]
    for copy in copies:
        copy.start()
    xs[:, WW:, :] = jnp.zeros((WH, PITCH - WW, xs.shape[-1]), F32)
    copies[0].wait()
    bias_strips(here[0], tab, strips)
    copies[1].wait()
    xs[:, :WW, :] = here[1][0].astype(F32)
    copies[2].wait()

    def weights(i):
        copies[3 + i].wait()
        return here[3 + i]

    attend(xs, ys, here[2], weights, strips, probs, None)
    quadrants(ys, (nw, ne, sw, se))


def second_kernel(nw_in, ne_in, sw_in, se_in, table, gain, wqkv, wproj, nw, ne, sw, se, xs, ys, tab, strips, probs):
    polar = lax.axis_index("lat") == lax.axis_size("lat") - 1
    xs[:, WW:, :] = jnp.zeros((WH, PITCH - WW, xs.shape[-1]), F32)
    at = 0
    pieces = (nw_in, ne_in, sw_in, se_in)
    for r in (0, HALF_R):
        for c in (0, HALF_C):
            xs[r : r + HALF_R, c : c + HALF_C, :] = pieces[at][...].astype(F32)
            at += 1
    bias_strips(table, tab, strips)
    attend(xs, ys, gain, lambda i: (wqkv, wproj)[i], strips, probs, polar)
    quadrants(ys, (nw, ne, sw, se))


def block(kernel, pieces, table, gain, wqkv, wproj, fetch):
    width = wproj.shape[0]
    heads, count = table.shape[1:]
    lanes = -(-count // LANES) * LANES
    group = LANES * heads // width
    piece = jax.ShapeDtypeStruct((HALF_R, HALF_C, width), BF16)
    args = (*pieces, table, gain.reshape(1, width), wqkv, wproj)
    vmem = pl.BlockSpec(memory_space=pltpu.VMEM)
    scratch = [
        pltpu.VMEM((WH, PITCH, width), F32),
        pltpu.VMEM((WH, PITCH, width), F32),
        pltpu.VMEM((heads, lanes), F32),
        pltpu.VMEM((heads, 2, SUB, 3 * LANES), F32),
        pltpu.VMEM((heads // group, WH * WW, group * WH * PITCH), BF16),
    ]
    if fetch:
        order = (args[1], args[0], *args[2:])
        scratch += [pltpu.VMEM(a.shape, a.dtype) for a in order]
        scratch += [pltpu.SemaphoreType.DMA((len(order),))]
        args = tuple(pltpu.with_memory_space_constraint(a, pltpu.HBM) for a in args)
    source = pl.BlockSpec(memory_space=pltpu.HBM) if fetch else vmem
    return pl.pallas_call(
        kernel,
        out_shape=(piece,) * 4,
        in_specs=[source] * len(args),
        out_specs=(vmem,) * 4,
        scratch_shapes=scratch,
        compiler_params=pltpu.CompilerParams(vmem_limit_bytes=24 << 20),
        cost_estimate=pl.CostEstimate(flops=400_000_000, bytes_accessed=2_500_000, transcendentals=600_000),
    )(*args)


def moved(piece, lat, lon):
    rows, cols = lax.axis_size("lat"), lax.axis_size("lon")
    route = [
        (((i + lat) % rows) * cols + (j + lon) % cols, i * cols + j) for i in range(rows) for j in range(cols)
    ]
    return lax.ppermute(piece, ("lat", "lon"), route)


def shards(
    tokens,
    gain_first,
    qkv_first,
    proj_first,
    bias_first,
    gain_second,
    qkv_second,
    proj_second,
    bias_second,
):
    nw, ne, sw, se = block(first_kernel, (tokens,), bias_first, gain_first, qkv_first, proj_first, True)
    window = (se, moved(sw, 0, 1), moved(ne, 1, 0), moved(nw, 1, 1))
    nw, ne, sw, se = block(second_kernel, window, bias_second, gain_second, qkv_second, proj_second, False)
    west, north, corner = moved(ne, 0, -1), moved(sw, -1, 0), moved(se, -1, -1)
    upper = jnp.concatenate([corner, north], axis=1)
    lower = jnp.concatenate([west, nw], axis=1)
    return jnp.concatenate([upper, lower], axis=0)[None]


def solution(mesh):
    placed = (
        P(None, "lat", "lon", None),
        P(),
        P(),
        P(),
        P("lat", None, None),
        P(),
        P(),
        P(),
        P("lat", None, None),
    )
    return jax.shard_map(
        shards, mesh=mesh, in_specs=placed, out_specs=P(None, "lat", "lon", None), check_vma=False
    )
```

```python
import functools

import jax
import jax.numpy as jnp
from jax import lax
from jax.experimental import pallas as pl
from jax.experimental.pallas import tpu as pltpu
from jax.sharding import PartitionSpec as P


HEADS = 16
WH = 12
WW = 12
LANES = 128
SUB = 8
PITCH = 16
SPAN_C = 2 * WW - 1
HALF_R = WH // 2
HALF_C = WW // 2
REST = WW - SUB
NEG = -1e30
F32 = jnp.float32
BF16 = jnp.bfloat16


def iota(shape, dim):
    return lax.broadcasted_iota(jnp.int32, shape, dim)


def bias_strips(table, tab, strips):
    heads = table.shape[1]
    count = table.shape[2]
    tab[...] = jnp.zeros_like(tab)
    tab[:, :count] = table[0]
    lane = iota((SUB, LANES), 1)
    row = iota((SUB, LANES), 0)
    plans = []
    for tile in range(2):
        for k in range(3):
            u = lane + k * LANES
            step = u // PITCH
            if tile == 0:
                col = row
            else:
                second = row >= REST
                col = SUB + jnp.where(second, row - REST, row)
                step = jnp.where(second, step - 1, step)
            index = step * SPAN_C + u % PITCH - col + WW - 1
            index = jnp.clip(index, 0, count - 1)
            low = max(8 * k - tile, 0) * SPAN_C
            top = min((8 * k + 7) * SPAN_C + PITCH + WW - 2, count - 1)
            sources = range(low // LANES, top // LANES + 1)
            plans.append((tile, k, index % LANES, index // LANES, sources))
    for h in range(heads):
        rows = {}
        for tile, k, inner, outer, sources in plans:
            value = None
            for s in sources:
                if s not in rows:
                    rows[s] = jnp.broadcast_to(tab[h : h + 1, s * LANES : (s + 1) * LANES], (SUB, LANES))
                taken = jnp.take_along_axis(rows[s], inner, axis=1)
                value = taken if value is None else jnp.where(outer == s, taken, value)
            strips[h, tile, :, k * LANES : (k + 1) * LANES] = value


def bias_tiles(strips, h):
    turned = {}
    lane = iota((SUB, LANES), 1)
    per_head = WH * PITCH

    def turn(head, tile, k, by):
        key = (head, tile, k, by)
        if key not in turned:
            part = strips[head, tile, :, k * LANES : (k + 1) * LANES]
            turned[key] = pltpu.roll(part, LANES - by, 1) if by else part
        return turned[key]

    def window(tile, start, t):
        cuts = []
        at = t * LANES
        while at < (t + 1) * LANES:
            which, query = divmod(at, per_head)
            u = start + query
            k = u // LANES
            end = min(at + (k + 1) * LANES - u, (which + 1) * per_head, (t + 1) * LANES)
            cuts.append((end - t * LANES, turn(h + which, tile, k, (u - at) % LANES)))
            at = end
        value = cuts[-1][1]
        for end, part in reversed(cuts[:-1]):
            value = jnp.where(lane < end, part, value)
        return value

    starts = [(0, PITCH * (WH - 1 - r)) for r in range(WH)]
    starts += [(1, PITCH * (WH - 1 - r)) for r in range(0, WH, 2)]
    return [[window(tile, start, t) for tile, start in starts] for t in range(2 * per_head // LANES)]


def halves(polar):
    lane = iota((SUB, LANES), 1)
    out = []
    for t in range(2 * WH * PITCH // LANES):
        query = (lane + t * LANES) % (WH * PITCH) // PITCH >= HALF_R
        out.append([jnp.where((query != lower) & polar, NEG, 0.0).astype(F32) for lower in (False, True)])
    return out


def compact(value):
    width = value.shape[-1]
    tiles = value.reshape(WH, 2, SUB, width)
    row = iota((SUB, width), 0)
    parts = [tiles[r, 0] for r in range(WH)]
    for r in range(0, WH, 2):
        parts.append(jnp.where(row < REST, tiles[r, 1], pltpu.roll(tiles[r + 1, 1], REST, 0)))
    return jnp.concatenate(parts, axis=0)


def split(value):
    high = value.astype(BF16)
    return high, (value - high.astype(F32)).astype(BF16)


def soft(scores, bias, mask, probs, at):
    count = len(bias)
    tiles = []
    for u in range(count):
        s = scores[u * SUB : (u + 1) * SUB] + bias[u]
        if mask is not None:
            lower = u >= HALF_R if u < WH else 2 * (u - WH) >= HALF_R
            s = s + mask[int(lower)]
        tiles.append(s)
    top = functools.reduce(jnp.maximum, tiles)
    top = jnp.max(top, axis=0, keepdims=True)
    tiles = [jnp.exp(s - top) for s in tiles]
    total = functools.reduce(jnp.add, tiles)
    inverse = 1.0 / jnp.sum(total, axis=0, keepdims=True)
    for u in range(0, count, 2):
        pair = jnp.concatenate([tiles[u] * inverse, tiles[u + 1] * inverse], axis=0)
        probs[u * SUB : (u + 2) * SUB, at : at + LANES] = pair.astype(BF16)


def attend(xs, ys, gain, weights, strips, probs, polar):
    width = xs.shape[-1]
    head_dim = width // HEADS
    group = LANES // head_dim
    per_head = WH * PITCH
    x = xs[...].reshape(per_head, width)
    mean = jnp.mean(x, axis=-1, keepdims=True)
    centred = x - mean
    var = jnp.mean(centred * centred, axis=-1, keepdims=True)
    normed = (centred * lax.rsqrt(var + 1e-05) * gain[...]).astype(BF16)
    wqkv = weights(0)
    mixed = jnp.dot(normed, wqkv[...], preferred_element_type=F32)
    q_hi, q_lo = split(mixed[:, :width] * head_dim ** (-0.5))
    k_hi, k_lo = split(compact(mixed[:, width : 2 * width]))
    values = compact(mixed[:, 2 * width :]).astype(BF16)
    lane = iota((1, LANES), 1)
    masks = None if polar is None else halves(polar)

    def product(g):
        part = slice(g * LANES, (g + 1) * LANES)
        left = jnp.concatenate([k_hi[:, part], k_hi[:, part], k_lo[:, part]], axis=1)
        rights = []
        for i in range(group):
            own = (lane // head_dim == i).astype(BF16)
            high = q_hi[:, part] * own
            rights.append(jnp.concatenate([high, q_lo[:, part] * own, high], axis=1))
        right = jnp.concatenate(rights, axis=0)
        return lax.dot_general(left, right, (((1,), (1,)), ((), ())), preferred_element_type=F32)

    outs = []
    groups = HEADS // group
    ahead = product(0)
    for g in range(groups):
        scores = ahead
        if g + 1 < groups:
            ahead = product(g + 1)
        for i in range(0, group, 2):
            bias = bias_tiles(strips, g * group + i)
            for t in range(len(bias)):
                at = i * per_head + t * LANES
                soft(scores[:, at : at + LANES], bias[t], masks and masks[t], probs.at[g], at)
        part = slice(g * LANES, (g + 1) * LANES)
        mixed_v = lax.dot_general(
            values[:, part], probs[g], (((0,), (0,)), ((), ())), preferred_element_type=F32
        )
        heads_out = []
        for i in range(group):
            rows = slice(i * head_dim, (i + 1) * head_dim)
            first, by = divmod(i * per_head, LANES)
            own = mixed_v[rows, first * LANES : (first + 2) * LANES]
            heads_out.append(pltpu.roll(own, 2 * LANES - by, 1) if by else own)
        outs.append(jnp.concatenate(heads_out, axis=0).T)
    heads_out = jnp.concatenate(outs, axis=1)[:per_head].astype(BF16)
    wproj = weights(1)
    branch = jnp.dot(heads_out, wproj[...], preferred_element_type=F32)
    ys[...] = xs[...] + branch.reshape(xs.shape)


def quadrants(ys, outs):
    at = 0
    for r in (0, HALF_R):
        for c in (0, HALF_C):
            outs[at][...] = ys[r : r + HALF_R, c : c + HALF_C, :].astype(BF16)
            at += 1


def edge(first):
    return lax.axis_index("lon") == (0 if first else lax.axis_size("lon") - 1)


def keep(mine, done, outs):
    @pl.when(mine)
    def _():
        for a, b in zip(done, outs):
            b[...] = a[...]


def first_kernel(early, *refs):
    tokens, table, gain, wqkv, wproj, *refs = refs
    if not early:
        done, refs = refs[:4], refs[4:]
    (nw, ne, sw, se), refs = refs[:4], refs[4:]
    if early:
        (nw_wrap, sw_wrap), refs = refs[:2], refs[2:]
    xs, ys, tab, strips, probs, *here, sems = refs
    mine = edge(True)

    @pl.when(mine if early else jnp.logical_not(mine))
    def _():
        copies = [
            pltpu.make_async_copy(a, b, sems.at[i])
            for i, (a, b) in enumerate(zip((table, tokens, gain, wqkv, wproj), here))
        ]
        for copy in copies:
            copy.start()
        xs[:, WW:, :] = jnp.zeros((WH, PITCH - WW, xs.shape[-1]), F32)
        copies[0].wait()
        bias_strips(here[0], tab, strips)
        copies[1].wait()
        xs[:, :WW, :] = here[1][0].astype(F32)
        copies[2].wait()

        def weights(i):
            copies[3 + i].wait()
            return here[3 + i]

        attend(xs, ys, here[2], weights, strips, probs, None)
        quadrants(ys, (nw, ne, sw, se))
        if early:
            nw_wrap[...] = nw[...]
            sw_wrap[...] = sw[...]

    if not early:
        keep(mine, done, (nw, ne, sw, se))


def second_kernel(early, *refs):
    nw_in, sw_in, ne_in, se_in, ne_wrap_in, se_wrap_in, table, gain, wqkv, wproj, *refs = refs
    if not early:
        done, refs = refs[:4], refs[4:]
    (nw, ne, sw, se), refs = refs[:4], refs[4:]
    if early:
        (ne_wrap, se_wrap), refs = refs[:2], refs[2:]
    xs, ys, tab, strips, probs = refs
    last = edge(False)
    polar = lax.axis_index("lat") == lax.axis_size("lat") - 1

    @pl.when(last if early else jnp.logical_not(last))
    def _():
        xs[:, WW:, :] = jnp.zeros((WH, PITCH - WW, xs.shape[-1]), F32)
        east = (ne_wrap_in, se_wrap_in) if early else (ne_in, se_in)
        pieces = (nw_in, east[0], sw_in, east[1])
        at = 0
        for r in (0, HALF_R):
            for c in (0, HALF_C):
                xs[r : r + HALF_R, c : c + HALF_C, :] = pieces[at][...].astype(F32)
                at += 1
        bias_strips(table, tab, strips)
        attend(xs, ys, gain, lambda i: (wqkv, wproj)[i], strips, probs, polar)
        quadrants(ys, (nw, ne, sw, se))
        if early:
            ne_wrap[...] = ne[...]
            se_wrap[...] = se[...]

    if not early:
        keep(last, done, (nw, ne, sw, se))


def block(kernel, pieces, table, gain, wqkv, wproj, fetch, done=()):
    width = wproj.shape[0]
    heads, count = table.shape[1:]
    lanes = -(-count // LANES) * LANES
    group = LANES * heads // width
    piece = jax.ShapeDtypeStruct((HALF_R, HALF_C, width), BF16)
    args = (*pieces, table, gain.reshape(1, width), wqkv, wproj)
    vmem = pl.BlockSpec(memory_space=pltpu.VMEM)
    scratch = [
        pltpu.VMEM((WH, PITCH, width), F32),
        pltpu.VMEM((WH, PITCH, width), F32),
        pltpu.VMEM((heads, lanes), F32),
        pltpu.VMEM((heads, 2, SUB, 3 * LANES), F32),
        pltpu.VMEM((heads // group, WH * WW, group * WH * PITCH), BF16),
    ]
    if fetch:
        order = (args[1], args[0], *args[2:])
        scratch += [pltpu.VMEM(a.shape, a.dtype) for a in order]
        scratch += [pltpu.SemaphoreType.DMA((len(order),))]
        args = tuple(pltpu.with_memory_space_constraint(a, pltpu.HBM) for a in args)
    source = pl.BlockSpec(memory_space=pltpu.HBM) if fetch else vmem
    outs = 4 if done else 6
    return pl.pallas_call(
        functools.partial(kernel, not done),
        out_shape=(piece,) * outs,
        in_specs=[source] * len(args) + [vmem] * len(done),
        out_specs=(vmem,) * outs,
        scratch_shapes=scratch,
        compiler_params=pltpu.CompilerParams(vmem_limit_bytes=24 << 20),
        cost_estimate=pl.CostEstimate(flops=400_000_000, bytes_accessed=2_500_000, transcendentals=600_000),
    )(*args, *done)


def moved(piece, lat, lon, wrap):
    rows, cols = lax.axis_size("lat"), lax.axis_size("lon")
    route = [
        (((i + lat) % rows) * cols + (j + lon) % cols, i * cols + j)
        for i in range(rows)
        for j in range(cols)
        if lon == 0 or (0 <= j + lon < cols) != wrap
    ]
    return lax.ppermute(piece, ("lat", "lon"), route)


def shards(
    tokens,
    gain_first,
    qkv_first,
    proj_first,
    bias_first,
    gain_second,
    qkv_second,
    proj_second,
    bias_second,
):
    first = (bias_first, gain_first, qkv_first, proj_first, True)
    second = (bias_second, gain_second, qkv_second, proj_second, False)
    *done, nw_wrap, sw_wrap = block(first_kernel, (tokens,), *first)
    east_wrap = moved(sw_wrap, 0, 1, True)
    corner_wrap = moved(nw_wrap, 1, 1, True)
    nw, ne, sw, se = block(first_kernel, (tokens,), *first, done)
    south = moved(ne, 1, 0, False)
    east = moved(sw, 0, 1, False)
    corner = moved(nw, 1, 1, False)
    window = (se, south, east, corner, east_wrap, corner_wrap)
    *done, ne_wrap, se_wrap = block(second_kernel, window, *second)
    west_wrap = moved(ne_wrap, 0, -1, True)
    corner_wrap = moved(se_wrap, -1, -1, True)
    nw, ne, sw, se = block(second_kernel, window, *second, done)
    north = moved(sw, -1, 0, False)
    west = moved(ne, 0, -1, False)
    corner = moved(se, -1, -1, False)
    head = edge(True)
    west = jnp.where(head, west_wrap, west)
    corner = jnp.where(head, corner_wrap, corner)
    upper = jnp.concatenate([corner, north], axis=1)
    lower = jnp.concatenate([west, nw], axis=1)
    return jnp.concatenate([upper, lower], axis=0)[None]


def solution(mesh):
    placed = (
        P(None, "lat", "lon", None),
        P(),
        P(),
        P(),
        P("lat", None, None),
        P(),
        P(),
        P(),
        P("lat", None, None),
    )
    return jax.shard_map(
        shards, mesh=mesh, in_specs=placed, out_specs=P(None, "lat", "lon", None), check_vma=False
    )
```

```python
import functools
import math

import jax
import jax.numpy as jnp
from jax import lax
from jax.experimental import pallas as pl
from jax.experimental.pallas import tpu as pltpu
from jax.sharding import PartitionSpec as P


HEADS = 16
WH = 12
WW = 12
LANES = 128
SUB = 8
PITCH = 16
SPAN_C = 2 * WW - 1
HALF_R = WH // 2
HALF_C = WW // 2
REST = WW - SUB
NEG = -1e30
LOG2E = math.log2(math.e)
F32 = jnp.float32
BF16 = jnp.bfloat16


def iota(shape, dim):
    return lax.broadcasted_iota(jnp.int32, shape, dim)


def bias_strips(table, tab, strips):
    heads = table.shape[1]
    count = table.shape[2]
    tab[...] = jnp.zeros_like(tab)
    tab[:, :count] = table[0]
    lane = iota((SUB, LANES), 1)
    row = iota((SUB, LANES), 0)
    plans = []
    for tile in range(2):
        for k in range(3):
            u = lane + k * LANES
            step = u // PITCH
            if tile == 0:
                col = row
            else:
                second = row >= REST
                col = SUB + jnp.where(second, row - REST, row)
                step = jnp.where(second, step - 1, step)
            index = step * SPAN_C + u % PITCH - col + WW - 1
            index = jnp.clip(index, 0, count - 1)
            low = max(8 * k - tile, 0) * SPAN_C
            top = min((8 * k + 7) * SPAN_C + PITCH + WW - 2, count - 1)
            sources = range(low // LANES, top // LANES + 1)
            plans.append((tile, k, index % LANES, index // LANES, sources))
    for h in range(heads):
        rows = {}
        for tile, k, inner, outer, sources in plans:
            value = None
            for s in sources:
                if s not in rows:
                    rows[s] = jnp.broadcast_to(tab[h : h + 1, s * LANES : (s + 1) * LANES], (SUB, LANES))
                taken = jnp.take_along_axis(rows[s], inner, axis=1)
                value = taken if value is None else jnp.where(outer == s, taken, value)
            strips[h, tile, :, k * LANES : (k + 1) * LANES] = value * LOG2E


def bias_tiles(strips, h):
    turned = {}
    lane = iota((SUB, LANES), 1)
    per_head = WH * PITCH

    def turn(head, tile, k, by):
        key = (head, tile, k, by)
        if key not in turned:
            part = strips[head, tile, :, k * LANES : (k + 1) * LANES]
            turned[key] = pltpu.roll(part, LANES - by, 1) if by else part
        return turned[key]

    def window(tile, start, t):
        cuts = []
        at = t * LANES
        while at < (t + 1) * LANES:
            which, query = divmod(at, per_head)
            u = start + query
            k = u // LANES
            end = min(at + (k + 1) * LANES - u, (which + 1) * per_head, (t + 1) * LANES)
            cuts.append((end - t * LANES, turn(h + which, tile, k, (u - at) % LANES)))
            at = end
        value = cuts[-1][1]
        for end, part in reversed(cuts[:-1]):
            value = jnp.where(lane < end, part, value)
        return value

    starts = [(0, PITCH * (WH - 1 - r)) for r in range(WH)]
    starts += [(1, PITCH * (WH - 1 - r)) for r in range(0, WH, 2)]
    return [[window(tile, start, t) for tile, start in starts] for t in range(2 * per_head // LANES)]


def halves(polar):
    lane = iota((SUB, LANES), 1)
    out = []
    for t in range(2 * WH * PITCH // LANES):
        query = (lane + t * LANES) % (WH * PITCH) // PITCH >= HALF_R
        out.append([jnp.where((query != lower) & polar, NEG, 0.0).astype(F32) for lower in (False, True)])
    return out


def compact(value):
    width = value.shape[-1]
    tiles = value.reshape(WH, 2, SUB, width)
    row = iota((SUB, width), 0)
    parts = [tiles[r, 0] for r in range(WH)]
    for r in range(0, WH, 2):
        parts.append(jnp.where(row < REST, tiles[r, 1], pltpu.roll(tiles[r + 1, 1], REST, 0)))
    return jnp.concatenate(parts, axis=0)


def split(value):
    high = value.astype(BF16)
    return high, (value - high.astype(F32)).astype(BF16)


def soft(scores, bias, mask, probs, at):
    count = len(bias)
    tiles = []
    for u in range(count):
        s = scores[u * SUB : (u + 1) * SUB] + bias[u]
        if mask is not None:
            lower = u >= HALF_R if u < WH else 2 * (u - WH) >= HALF_R
            s = s + mask[int(lower)]
        tiles.append(s)
    top = functools.reduce(jnp.maximum, tiles)
    top = jnp.max(top, axis=0, keepdims=True)
    tiles = [jnp.exp2(s - top) for s in tiles]
    total = functools.reduce(jnp.add, tiles)
    inverse = 1.0 / jnp.sum(total, axis=0, keepdims=True)
    for u in range(0, count, 2):
        pair = jnp.concatenate([tiles[u] * inverse, tiles[u + 1] * inverse], axis=0)
        probs[u * SUB : (u + 2) * SUB, at : at + LANES] = pair.astype(BF16)


def attend(xs, ys, gain, weights, bias, probs, polar):
    width = xs.shape[-1]
    head_dim = width // HEADS
    group = LANES // head_dim
    per_head = WH * PITCH
    tiles_of = bias()
    x = xs[...].reshape(per_head, width)
    mean = jnp.mean(x, axis=-1, keepdims=True)
    centred = x - mean
    var = jnp.mean(centred * centred, axis=-1, keepdims=True)
    normed = (centred * lax.rsqrt(var + 1e-05) * gain[...]).astype(BF16)
    wqkv = weights(0)
    mixed = jnp.dot(normed, wqkv[...], preferred_element_type=F32)
    q_hi, q_lo = split(mixed[:, :width] * (head_dim ** (-0.5) * LOG2E))
    k_hi, k_lo = split(compact(mixed[:, width : 2 * width]))
    values = compact(mixed[:, 2 * width :]).astype(BF16)
    lane = iota((1, LANES), 1)
    masks = None if polar is None else halves(polar)

    def product(g):
        part = slice(g * LANES, (g + 1) * LANES)
        left = jnp.concatenate([k_hi[:, part], k_hi[:, part], k_lo[:, part]], axis=1)
        rights = []
        for i in range(group):
            own = (lane // head_dim == i).astype(BF16)
            high = q_hi[:, part] * own
            rights.append(jnp.concatenate([high, q_lo[:, part] * own, high], axis=1))
        right = jnp.concatenate(rights, axis=0)
        return lax.dot_general(left, right, (((1,), (1,)), ((), ())), preferred_element_type=F32)

    def gather(g):
        part = slice(g * LANES, (g + 1) * LANES)
        mixed_v = lax.dot_general(
            values[:, part], probs[g], (((0,), (0,)), ((), ())), preferred_element_type=F32
        )
        heads_out = []
        for i in range(group):
            rows = slice(i * head_dim, (i + 1) * head_dim)
            first, by = divmod(i * per_head, LANES)
            own = mixed_v[rows, first * LANES : (first + 2) * LANES]
            heads_out.append(pltpu.roll(own, 2 * LANES - by, 1) if by else own)
        return jnp.concatenate(heads_out, axis=0).T

    outs = []
    groups = HEADS // group
    ahead = product(0)
    for g in range(groups):
        scores = ahead
        if g + 1 < groups:
            ahead = product(g + 1)
        if g:
            outs.append(gather(g - 1))
        for i in range(0, group, 2):
            tiles = tiles_of(g * group + i)
            for t in range(len(tiles)):
                at = i * per_head + t * LANES
                soft(scores[:, at : at + LANES], tiles[t], masks and masks[t], probs.at[g], at)
    outs.append(gather(groups - 1))
    heads_out = jnp.concatenate(outs, axis=1)[:per_head].astype(BF16)
    wproj = weights(1)
    branch = jnp.dot(heads_out, wproj[...], preferred_element_type=F32)
    ys[...] = xs[...] + branch.reshape(xs.shape)


def quadrants(ys, outs):
    at = 0
    for r in (0, HALF_R):
        for c in (0, HALF_C):
            outs[at][...] = ys[r : r + HALF_R, c : c + HALF_C, :].astype(BF16)
            at += 1


def first_kernel(tokens, table, gain, wqkv, wproj, nw, ne, sw, se, xs, ys, probs, tab, strips, *here):
    here, sems = here[:-1], here[-1]
    copies = [
        pltpu.make_async_copy(a, b, sems.at[i])
        for i, (a, b) in enumerate(zip((tokens, gain, wqkv, table, wproj), here))
    ]
    for copy in copies:
        copy.start()
    xs[:, WW:, :] = jnp.zeros((WH, PITCH - WW, xs.shape[-1]), F32)
    copies[0].wait()
    xs[:, :WW, :] = here[0][0].astype(F32)
    copies[1].wait()

    def weights(i):
        copies[2 * i + 2].wait()
        return here[2 * i + 2]

    def bias():
        copies[3].wait()
        bias_strips(here[3], tab, strips)
        return functools.partial(bias_tiles, strips)

    attend(xs, ys, here[1], weights, bias, probs, None)
    quadrants(ys, (nw, ne, sw, se))


def bias_kernel(table, out, tab, strips):
    bias_strips(table, tab, strips)
    for pair in range(out.shape[0]):
        for t, tiles in enumerate(bias_tiles(strips, 2 * pair)):
            for u, tile in enumerate(tiles):
                out[pair, t, u] = tile


def second_kernel(nw_in, ne_in, sw_in, se_in, bias, gain, wqkv, wproj, nw, ne, sw, se, xs, ys, probs):
    polar = lax.axis_index("lat") == lax.axis_size("lat") - 1
    xs[:, WW:, :] = jnp.zeros((WH, PITCH - WW, xs.shape[-1]), F32)
    at = 0
    pieces = (nw_in, ne_in, sw_in, se_in)
    for r in (0, HALF_R):
        for c in (0, HALF_C):
            xs[r : r + HALF_R, c : c + HALF_C, :] = pieces[at][...].astype(F32)
            at += 1

    def tiles_of(h):
        return [[bias[h // 2, t, u] for u in range(bias.shape[2])] for t in range(bias.shape[1])]

    attend(xs, ys, gain, lambda i: (wqkv, wproj)[i], lambda: tiles_of, probs, polar)
    quadrants(ys, (nw, ne, sw, se))


VMEM = pl.BlockSpec(memory_space=pltpu.VMEM)


def bias_room(table):
    _, heads, count = table.shape
    lanes = -(-count // LANES) * LANES
    return [pltpu.VMEM((heads, lanes), F32), pltpu.VMEM((heads, 2, SUB, 3 * LANES), F32)]


def expand(table):
    heads = table.shape[1]
    lane_tiles = 2 * WH * PITCH // LANES
    shape = (heads // 2, lane_tiles, WH * WW // SUB, SUB, LANES)
    return pl.pallas_call(
        bias_kernel,
        out_shape=jax.ShapeDtypeStruct(shape, F32),
        in_specs=[VMEM],
        out_specs=VMEM,
        scratch_shapes=bias_room(table),
        compiler_params=pltpu.CompilerParams(vmem_limit_bytes=8 << 20),
        cost_estimate=pl.CostEstimate(flops=2_000_000, bytes_accessed=1_800_000, transcendentals=0),
    )(table)


def block(kernel, pieces, bias, gain, wqkv, wproj, fetch):
    width = wproj.shape[0]
    group = LANES * HEADS // width
    piece = jax.ShapeDtypeStruct((HALF_R, HALF_C, width), BF16)
    args = (*pieces, bias, gain.reshape(1, width), wqkv, wproj)
    scratch = [
        pltpu.VMEM((WH, PITCH, width), F32),
        pltpu.VMEM((WH, PITCH, width), F32),
        pltpu.VMEM((HEADS // group, WH * WW, group * WH * PITCH), BF16),
    ]
    if fetch:
        order = (args[0], args[2], args[3], args[1], args[4])
        scratch += bias_room(bias)
        scratch += [pltpu.VMEM(a.shape, a.dtype) for a in order]
        scratch += [pltpu.SemaphoreType.DMA((len(order),))]
        args = tuple(pltpu.with_memory_space_constraint(a, pltpu.HBM) for a in args)
    source = pl.BlockSpec(memory_space=pltpu.HBM) if fetch else VMEM
    return pl.pallas_call(
        kernel,
        out_shape=(piece,) * 4,
        in_specs=[source] * len(args),
        out_specs=(VMEM,) * 4,
        scratch_shapes=scratch,
        compiler_params=pltpu.CompilerParams(vmem_limit_bytes=24 << 20),
        cost_estimate=pl.CostEstimate(flops=400_000_000, bytes_accessed=2_500_000, transcendentals=600_000),
    )(*args)


def moved(piece, lat, lon):
    rows, cols = lax.axis_size("lat"), lax.axis_size("lon")
    route = [
        (((i + lat) % rows) * cols + (j + lon) % cols, i * cols + j) for i in range(rows) for j in range(cols)
    ]
    return lax.ppermute(piece, ("lat", "lon"), route)


def shards(
    tokens,
    gain_first,
    qkv_first,
    proj_first,
    bias_first,
    gain_second,
    qkv_second,
    proj_second,
    bias_second,
):
    nw, ne, sw, se = block(first_kernel, (tokens,), bias_first, gain_first, qkv_first, proj_first, True)
    sw, qkv_second, proj_second, bias_second = lax.optimization_barrier(
        (sw, qkv_second, proj_second, bias_second)
    )
    bias = expand(bias_second)
    east = moved(sw, 0, 1)
    south = moved(ne, 1, 0)
    corner = moved(nw, 1, 1)
    window = (se, east, south, corner)
    nw, ne, sw, se = block(second_kernel, window, bias, gain_second, qkv_second, proj_second, False)
    west, north, corner = moved(ne, 0, -1), moved(sw, -1, 0), moved(se, -1, -1)
    upper = jnp.concatenate([corner, north], axis=1)
    lower = jnp.concatenate([west, nw], axis=1)
    return jnp.concatenate([upper, lower], axis=0)[None]


def solution(mesh):
    placed = (
        P(None, "lat", "lon", None),
        P(),
        P(),
        P(),
        P("lat", None, None),
        P(),
        P(),
        P(),
        P("lat", None, None),
    )
    return jax.shard_map(
        shards, mesh=mesh, in_specs=placed, out_specs=P(None, "lat", "lon", None), check_vma=False
    )
```

```python
import functools
import math

import jax
import jax.numpy as jnp
from jax import lax
from jax.experimental import pallas as pl
from jax.experimental.pallas import tpu as pltpu
from jax.sharding import PartitionSpec as P


HEADS = 16
CUTS = 4
CUT_FROM = 1 << 19
WH = 12
WW = 12
LANES = 128
SUB = 8
PITCH = 16
SPAN_C = 2 * WW - 1
HALF_R = WH // 2
HALF_C = WW // 2
REST = WW - SUB
NEG = -1e30
LOG2E = math.log2(math.e)
F32 = jnp.float32
BF16 = jnp.bfloat16


def iota(shape, dim):
    return lax.broadcasted_iota(jnp.int32, shape, dim)


def bias_strips(table, tab, strips):
    heads = table.shape[1]
    count = table.shape[2]
    tab[...] = jnp.zeros_like(tab)
    tab[:, :count] = table[0]
    lane = iota((SUB, LANES), 1)
    row = iota((SUB, LANES), 0)
    plans = []
    for tile in range(2):
        for k in range(3):
            u = lane + k * LANES
            step = u // PITCH
            if tile == 0:
                col = row
            else:
                second = row >= REST
                col = SUB + jnp.where(second, row - REST, row)
                step = jnp.where(second, step - 1, step)
            index = step * SPAN_C + u % PITCH - col + WW - 1
            index = jnp.clip(index, 0, count - 1)
            low = max(8 * k - tile, 0) * SPAN_C
            top = min((8 * k + 7) * SPAN_C + PITCH + WW - 2, count - 1)
            sources = range(low // LANES, top // LANES + 1)
            plans.append((tile, k, index % LANES, index // LANES, sources))
    for tile, k, inner, outer, sources in plans:
        values = [None] * heads
        for s in sources:
            here = outer == s
            for h in range(heads):
                row = jnp.broadcast_to(tab[h : h + 1, s * LANES : (s + 1) * LANES], (SUB, LANES))
                taken = jnp.take_along_axis(row, inner, axis=1)
                values[h] = taken if values[h] is None else jnp.where(here, taken, values[h])
        for h in range(heads):
            strips[h, tile, :, k * LANES : (k + 1) * LANES] = values[h] * LOG2E


def bias_tiles(strips, h):
    turned = {}
    lane = iota((SUB, LANES), 1)
    per_head = WH * PITCH

    def turn(head, tile, k, by):
        key = (head, tile, k, by)
        if key not in turned:
            part = strips[head, tile, :, k * LANES : (k + 1) * LANES]
            turned[key] = pltpu.roll(part, LANES - by, 1) if by else part
        return turned[key]

    def window(tile, start, t):
        cuts = []
        at = t * LANES
        while at < (t + 1) * LANES:
            which, query = divmod(at, per_head)
            u = start + query
            k = u // LANES
            end = min(at + (k + 1) * LANES - u, (which + 1) * per_head, (t + 1) * LANES)
            cuts.append((end - t * LANES, turn(h + which, tile, k, (u - at) % LANES)))
            at = end
        value = cuts[-1][1]
        for end, part in reversed(cuts[:-1]):
            value = jnp.where(lane < end, part, value)
        return value

    starts = [(0, PITCH * (WH - 1 - r)) for r in range(WH)]
    starts += [(1, PITCH * (WH - 1 - r)) for r in range(0, WH, 2)]
    return [[window(tile, start, t) for tile, start in starts] for t in range(2 * per_head // LANES)]


def halves(polar):
    lane = iota((SUB, LANES), 1)
    out = []
    for t in range(2 * WH * PITCH // LANES):
        query = (lane + t * LANES) % (WH * PITCH) // PITCH >= HALF_R
        out.append([jnp.where((query != lower) & polar, NEG, 0.0).astype(F32) for lower in (False, True)])
    return out


def compact(value):
    width = value.shape[-1]
    tiles = value.reshape(WH, 2, SUB, width)
    row = iota((SUB, width), 0)
    parts = [tiles[r, 0] for r in range(WH)]
    for r in range(0, WH, 2):
        parts.append(jnp.where(row < REST, tiles[r, 1], pltpu.roll(tiles[r + 1, 1], REST, 0)))
    return jnp.concatenate(parts, axis=0)


def split(value):
    high = value.astype(BF16)
    return high, (value - high.astype(F32)).astype(BF16)


def soft(scores, bias, mask, probs, at):
    count = len(bias)
    tiles = []
    for u in range(count):
        s = scores[u * SUB : (u + 1) * SUB] + bias[u]
        if mask is not None:
            lower = u >= HALF_R if u < WH else 2 * (u - WH) >= HALF_R
            s = s + mask[int(lower)]
        tiles.append(s)
    top = functools.reduce(jnp.maximum, tiles)
    top = jnp.max(top, axis=0, keepdims=True)
    tiles = [jnp.exp2(s - top) for s in tiles]
    total = functools.reduce(jnp.add, tiles)
    inverse = 1.0 / jnp.sum(total, axis=0, keepdims=True)
    for u in range(0, count, 2):
        pair = jnp.concatenate([tiles[u] * inverse, tiles[u + 1] * inverse], axis=0)
        probs[u * SUB : (u + 2) * SUB, at : at + LANES] = pair.astype(BF16)


def attend(xs, ys, gain, weights, tiles_of, probs, polar):
    width = xs.shape[-1]
    head_dim = width // HEADS
    group = LANES // head_dim
    per_head = WH * PITCH
    x = xs[...].reshape(per_head, width)
    mean = jnp.mean(x, axis=-1, keepdims=True)
    centred = x - mean
    var = jnp.mean(centred * centred, axis=-1, keepdims=True)
    normed = (centred * lax.rsqrt(var + 1e-05) * gain[...]).astype(BF16)
    wqkv = weights(0)
    mixed = jnp.dot(normed, wqkv[...], preferred_element_type=F32)
    q_hi, q_lo = split(mixed[:, :width] * (head_dim ** (-0.5) * LOG2E))
    k_hi, k_lo = split(compact(mixed[:, width : 2 * width]))
    values = compact(mixed[:, 2 * width :]).astype(BF16)
    lane = iota((1, LANES), 1)
    masks = None if polar is None else halves(polar)

    def product(g):
        part = slice(g * LANES, (g + 1) * LANES)
        left = jnp.concatenate([k_hi[:, part], k_hi[:, part], k_lo[:, part]], axis=1)
        rights = []
        for i in range(group):
            own = (lane // head_dim == i).astype(BF16)
            high = q_hi[:, part] * own
            rights.append(jnp.concatenate([high, q_lo[:, part] * own, high], axis=1))
        right = jnp.concatenate(rights, axis=0)
        return lax.dot_general(left, right, (((1,), (1,)), ((), ())), preferred_element_type=F32)

    def gather(g):
        part = slice(g * LANES, (g + 1) * LANES)
        mixed_v = lax.dot_general(
            values[:, part], probs[g], (((0,), (0,)), ((), ())), preferred_element_type=F32
        )
        heads_out = []
        for i in range(group):
            rows = slice(i * head_dim, (i + 1) * head_dim)
            first, by = divmod(i * per_head, LANES)
            own = mixed_v[rows, first * LANES : (first + 2) * LANES]
            heads_out.append(pltpu.roll(own, 2 * LANES - by, 1) if by else own)
        return jnp.concatenate(heads_out, axis=0).T

    outs = []
    groups = HEADS // group
    ahead = product(0)
    for g in range(groups):
        scores = ahead
        if g + 1 < groups:
            ahead = product(g + 1)
        if g:
            outs.append(gather(g - 1))
        for i in range(0, group, 2):
            tiles = tiles_of(g * group + i)
            for t in range(len(tiles)):
                at = i * per_head + t * LANES
                soft(scores[:, at : at + LANES], tiles[t], masks and masks[t], probs.at[g], at)
    outs.append(gather(groups - 1))
    heads_out = jnp.concatenate(outs, axis=1)[:per_head].astype(BF16)
    wproj = weights(1)
    branch = jnp.dot(heads_out, wproj[...], preferred_element_type=F32)
    ys[...] = xs[...] + branch.reshape(xs.shape)


def quadrants(ys, outs):
    at = 0
    for r in (0, HALF_R):
        for c in (0, HALF_C):
            outs[at][...] = ys[r : r + HALF_R, c : c + HALF_C, :].astype(BF16)
            at += 1


def cuts(shape):
    if len(shape) == 2 and shape[0] * shape[1] >= CUT_FROM:
        rows = shape[0] // CUTS
        return [pl.ds(i * rows, rows) for i in range(CUTS)]
    return [slice(None)]


def pieces_of(source, target):
    return [(source.at[part], target.at[part]) for part in cuts(source.shape)]


def first_kernel(tokens, table, gain, wqkv, wproj, nw, ne, sw, se, xs, ys, probs, tab, strips, *here):
    here, sems = here[:-1], here[-1]
    pairs = [pair for a, b in zip((table, tokens, gain, wqkv, wproj), here) for pair in pieces_of(a, b)]
    copies = [pltpu.make_async_copy(a, b, sems.at[i]) for i, (a, b) in enumerate(pairs)]
    for copy in copies:
        copy.start()
    xs[:, WW:, :] = jnp.zeros((WH, PITCH - WW, xs.shape[-1]), F32)
    copies[0].wait()
    bias_strips(here[0], tab, strips)
    copies[1].wait()
    xs[:, :WW, :] = here[1][0].astype(F32)
    copies[2].wait()

    def weights(i):
        for copy in (copies[3:-1], copies[-1:])[i]:
            copy.wait()
        return here[3 + i]

    attend(xs, ys, here[2], weights, functools.partial(bias_tiles, strips), probs, None)
    quadrants(ys, (nw, ne, sw, se))


def bias_kernel(table, wqkv, wproj, out, wqkv_out, wproj_out, tab, strips, sems):
    pairs = pieces_of(wqkv, wqkv_out) + pieces_of(wproj, wproj_out)
    copies = [pltpu.make_async_copy(a, b, sems.at[i]) for i, (a, b) in enumerate(pairs)]
    for copy in copies:
        copy.start()
    bias_strips(table, tab, strips)
    for pair in range(out.shape[0]):
        for t, tiles in enumerate(bias_tiles(strips, 2 * pair)):
            for u, tile in enumerate(tiles):
                out[pair, t, u] = tile
    for copy in copies:
        copy.wait()


def second_kernel(nw_in, ne_in, sw_in, se_in, bias, gain, wqkv, wproj, nw, ne, sw, se, xs, ys, probs):
    polar = lax.axis_index("lat") == lax.axis_size("lat") - 1
    xs[:, WW:, :] = jnp.zeros((WH, PITCH - WW, xs.shape[-1]), F32)
    at = 0
    pieces = (nw_in, ne_in, sw_in, se_in)
    for r in (0, HALF_R):
        for c in (0, HALF_C):
            xs[r : r + HALF_R, c : c + HALF_C, :] = pieces[at][...].astype(F32)
            at += 1

    def tiles_of(h):
        return [[bias[h // 2, t, u] for u in range(bias.shape[2])] for t in range(bias.shape[1])]

    attend(xs, ys, gain, lambda i: (wqkv, wproj)[i], tiles_of, probs, polar)
    quadrants(ys, (nw, ne, sw, se))


VMEM = pl.BlockSpec(memory_space=pltpu.VMEM)
HBM = pl.BlockSpec(memory_space=pltpu.HBM)


def bias_room(table):
    _, heads, count = table.shape
    lanes = -(-count // LANES) * LANES
    return [pltpu.VMEM((heads, lanes), F32), pltpu.VMEM((heads, 2, SUB, 3 * LANES), F32)]


def expand(table, wqkv, wproj):
    heads = table.shape[1]
    lane_tiles = 2 * WH * PITCH // LANES
    shape = (heads // 2, lane_tiles, WH * WW // SUB, SUB, LANES)
    return pl.pallas_call(
        bias_kernel,
        out_shape=(
            jax.ShapeDtypeStruct(shape, F32),
            jax.ShapeDtypeStruct(wqkv.shape, wqkv.dtype),
            jax.ShapeDtypeStruct(wproj.shape, wproj.dtype),
        ),
        in_specs=[VMEM, HBM, HBM],
        out_specs=(VMEM,) * 3,
        scratch_shapes=bias_room(table)
        + [pltpu.SemaphoreType.DMA((len(cuts(wqkv.shape)) + len(cuts(wproj.shape)),))],
        compiler_params=pltpu.CompilerParams(vmem_limit_bytes=8 << 20),
        cost_estimate=pl.CostEstimate(flops=2_000_000, bytes_accessed=1_800_000, transcendentals=0),
    )(table, *(pltpu.with_memory_space_constraint(a, pltpu.HBM) for a in (wqkv, wproj)))


def block(kernel, pieces, bias, gain, wqkv, wproj, fetch):
    width = wproj.shape[0]
    group = LANES * HEADS // width
    piece = jax.ShapeDtypeStruct((HALF_R, HALF_C, width), BF16)
    args = (*pieces, bias, gain.reshape(1, width), wqkv, wproj)
    scratch = [
        pltpu.VMEM((WH, PITCH, width), F32),
        pltpu.VMEM((WH, PITCH, width), F32),
        pltpu.VMEM((HEADS // group, WH * WW, group * WH * PITCH), BF16),
    ]
    if fetch:
        order = (args[1], args[0], *args[2:])
        scratch += bias_room(bias)
        scratch += [pltpu.VMEM(a.shape, a.dtype) for a in order]
        scratch += [pltpu.SemaphoreType.DMA((sum(len(cuts(a.shape)) for a in order),))]
        args = tuple(pltpu.with_memory_space_constraint(a, pltpu.HBM) for a in args)
    source = HBM if fetch else VMEM
    return pl.pallas_call(
        kernel,
        out_shape=(piece,) * 4,
        in_specs=[source] * len(args),
        out_specs=(VMEM,) * 4,
        scratch_shapes=scratch,
        compiler_params=pltpu.CompilerParams(vmem_limit_bytes=24 << 20),
        cost_estimate=pl.CostEstimate(flops=400_000_000, bytes_accessed=2_500_000, transcendentals=600_000),
    )(*args)


def moved(piece, lat, lon):
    rows, cols = lax.axis_size("lat"), lax.axis_size("lon")
    route = [
        (((i + lat) % rows) * cols + (j + lon) % cols, i * cols + j) for i in range(rows) for j in range(cols)
    ]
    return lax.ppermute(piece, ("lat", "lon"), route)


def shards(
    tokens,
    gain_first,
    qkv_first,
    proj_first,
    bias_first,
    gain_second,
    qkv_second,
    proj_second,
    bias_second,
):
    nw, ne, sw, se = block(first_kernel, (tokens,), bias_first, gain_first, qkv_first, proj_first, True)
    bias, qkv_second, proj_second = expand(bias_second, qkv_second, proj_second)
    window = (se, moved(sw, 0, 1), moved(ne, 1, 0), moved(nw, 1, 1))
    nw, ne, sw, se = block(second_kernel, window, bias, gain_second, qkv_second, proj_second, False)
    west, north, corner = moved(ne, 0, -1), moved(sw, -1, 0), moved(se, -1, -1)
    upper = jnp.concatenate([corner, north], axis=1)
    lower = jnp.concatenate([west, nw], axis=1)
    return jnp.concatenate([upper, lower], axis=0)[None]


def solution(mesh):
    placed = (
        P(None, "lat", "lon", None),
        P(),
        P(),
        P(),
        P("lat", None, None),
        P(),
        P(),
        P(),
        P("lat", None, None),
    )
    return jax.shard_map(
        shards, mesh=mesh, in_specs=placed, out_specs=P(None, "lat", "lon", None), check_vma=False
    )
```

```python
import functools
import math

import jax
import jax.numpy as jnp
from jax import lax
from jax.experimental import pallas as pl
from jax.experimental.pallas import tpu as pltpu
from jax.sharding import PartitionSpec as P


HEADS = 16
NEXT = 2
CUTS = 4
CUT_FROM = 1 << 19
WH = 12
WW = 12
LANES = 128
SUB = 8
PITCH = 16
SPAN_C = 2 * WW - 1
HALF_R = WH // 2
HALF_C = WW // 2
REST = WW - SUB
NEG = -1e30
LOG2E = math.log2(math.e)
F32 = jnp.float32
BF16 = jnp.bfloat16


def iota(shape, dim):
    return lax.broadcasted_iota(jnp.int32, shape, dim)


def bias_strips(table, tab, strips):
    heads = table.shape[1]
    count = table.shape[2]
    tab[...] = jnp.zeros_like(tab)
    tab[:, :count] = table[0]
    lane = iota((SUB, LANES), 1)
    row = iota((SUB, LANES), 0)
    plans = []
    for tile in range(2):
        for k in range(3):
            u = lane + k * LANES
            step = u // PITCH
            if tile == 0:
                col = row
            else:
                second = row >= REST
                col = SUB + jnp.where(second, row - REST, row)
                step = jnp.where(second, step - 1, step)
            index = step * SPAN_C + u % PITCH - col + WW - 1
            index = jnp.clip(index, 0, count - 1)
            low = max(8 * k - tile, 0) * SPAN_C
            top = min((8 * k + 7) * SPAN_C + PITCH + WW - 2, count - 1)
            sources = range(low // LANES, top // LANES + 1)
            plans.append((tile, k, index % LANES, index // LANES, sources))
    for tile, k, inner, outer, sources in plans:
        values = [None] * heads
        for s in sources:
            here = outer == s
            for h in range(heads):
                row = jnp.broadcast_to(tab[h : h + 1, s * LANES : (s + 1) * LANES], (SUB, LANES))
                taken = jnp.take_along_axis(row, inner, axis=1)
                values[h] = taken if values[h] is None else jnp.where(here, taken, values[h])
        for h in range(heads):
            strips[h, tile, :, k * LANES : (k + 1) * LANES] = values[h] * LOG2E


def bias_tiles(strips, h):
    turned = {}
    lane = iota((SUB, LANES), 1)
    per_head = WH * PITCH

    def turn(head, tile, k, by):
        key = (head, tile, k, by)
        if key not in turned:
            part = strips[head, tile, :, k * LANES : (k + 1) * LANES]
            turned[key] = pltpu.roll(part, LANES - by, 1) if by else part
        return turned[key]

    def window(tile, start, t):
        cuts = []
        at = t * LANES
        while at < (t + 1) * LANES:
            which, query = divmod(at, per_head)
            u = start + query
            k = u // LANES
            end = min(at + (k + 1) * LANES - u, (which + 1) * per_head, (t + 1) * LANES)
            cuts.append((end - t * LANES, turn(h + which, tile, k, (u - at) % LANES)))
            at = end
        value = cuts[-1][1]
        for end, part in reversed(cuts[:-1]):
            value = jnp.where(lane < end, part, value)
        return value

    starts = [(0, PITCH * (WH - 1 - r)) for r in range(WH)]
    starts += [(1, PITCH * (WH - 1 - r)) for r in range(0, WH, 2)]
    return [[window(tile, start, t) for tile, start in starts] for t in range(2 * per_head // LANES)]


def halves(polar):
    lane = iota((SUB, LANES), 1)
    out = []
    for t in range(2 * WH * PITCH // LANES):
        query = (lane + t * LANES) % (WH * PITCH) // PITCH >= HALF_R
        out.append([jnp.where((query != lower) & polar, NEG, 0.0).astype(F32) for lower in (False, True)])
    return out


def compact(value):
    width = value.shape[-1]
    tiles = value.reshape(WH, 2, SUB, width)
    row = iota((SUB, width), 0)
    parts = [tiles[r, 0] for r in range(WH)]
    for r in range(0, WH, 2):
        parts.append(jnp.where(row < REST, tiles[r, 1], pltpu.roll(tiles[r + 1, 1], REST, 0)))
    return jnp.concatenate(parts, axis=0)


def split(value):
    high = value.astype(BF16)
    return high, (value - high.astype(F32)).astype(BF16)


def soft(scores, bias, mask, probs, at):
    count = len(bias)
    tiles = []
    for u in range(count):
        s = scores[u * SUB : (u + 1) * SUB] + bias[u]
        if mask is not None:
            lower = u >= HALF_R if u < WH else 2 * (u - WH) >= HALF_R
            s = s + mask[int(lower)]
        tiles.append(s)
    top = functools.reduce(jnp.maximum, tiles)
    top = jnp.max(top, axis=0, keepdims=True)
    tiles = [jnp.exp2(s - top) for s in tiles]
    total = functools.reduce(jnp.add, tiles)
    inverse = 1.0 / jnp.sum(total, axis=0, keepdims=True)
    for u in range(0, count, 2):
        pair = jnp.concatenate([tiles[u] * inverse, tiles[u + 1] * inverse], axis=0)
        probs[u * SUB : (u + 2) * SUB, at : at + LANES] = pair.astype(BF16)


def attend(xs, ys, gain, weights, tiles_of, probs, polar):
    width = xs.shape[-1]
    head_dim = width // HEADS
    group = LANES // head_dim
    per_head = WH * PITCH
    x = xs[...].reshape(per_head, width)
    mean = jnp.mean(x, axis=-1, keepdims=True)
    centred = x - mean
    var = jnp.mean(centred * centred, axis=-1, keepdims=True)
    normed = (centred * lax.rsqrt(var + 1e-05) * gain[...]).astype(BF16)
    wqkv = weights(0)
    mixed = jnp.dot(normed, wqkv[...], preferred_element_type=F32)
    q_hi, q_lo = split(mixed[:, :width] * (head_dim ** (-0.5) * LOG2E))
    k_hi, k_lo = split(compact(mixed[:, width : 2 * width]))
    values = compact(mixed[:, 2 * width :]).astype(BF16)
    lane = iota((1, LANES), 1)
    masks = None if polar is None else halves(polar)

    def product(g):
        part = slice(g * LANES, (g + 1) * LANES)
        left = jnp.concatenate([k_hi[:, part], k_hi[:, part], k_lo[:, part]], axis=1)
        rights = []
        for i in range(group):
            own = (lane // head_dim == i).astype(BF16)
            high = q_hi[:, part] * own
            rights.append(jnp.concatenate([high, q_lo[:, part] * own, high], axis=1))
        right = jnp.concatenate(rights, axis=0)
        return lax.dot_general(left, right, (((1,), (1,)), ((), ())), preferred_element_type=F32)

    def gather(g):
        part = slice(g * LANES, (g + 1) * LANES)
        mixed_v = lax.dot_general(
            values[:, part], probs[g], (((0,), (0,)), ((), ())), preferred_element_type=F32
        )
        heads_out = []
        for i in range(group):
            rows = slice(i * head_dim, (i + 1) * head_dim)
            first, by = divmod(i * per_head, LANES)
            own = mixed_v[rows, first * LANES : (first + 2) * LANES]
            heads_out.append(pltpu.roll(own, 2 * LANES - by, 1) if by else own)
        return jnp.concatenate(heads_out, axis=0).T

    outs = []
    groups = HEADS // group
    ahead = product(0)
    for g in range(groups):
        scores = ahead
        if g + 1 < groups:
            ahead = product(g + 1)
        if g:
            outs.append(gather(g - 1))
        for i in range(0, group, 2):
            tiles = tiles_of(g * group + i)
            for t in range(len(tiles)):
                at = i * per_head + t * LANES
                soft(scores[:, at : at + LANES], tiles[t], masks and masks[t], probs.at[g], at)
    outs.append(gather(groups - 1))
    heads_out = jnp.concatenate(outs, axis=1)[:per_head].astype(BF16)
    wproj = weights(1)
    branch = jnp.dot(heads_out, wproj[...], preferred_element_type=F32)
    ys[...] = xs[...] + branch.reshape(xs.shape)


def quadrants(ys, outs):
    at = 0
    for r in (0, HALF_R):
        for c in (0, HALF_C):
            outs[at][...] = ys[r : r + HALF_R, c : c + HALF_C, :].astype(BF16)
            at += 1


def cuts(shape):
    if len(shape) == 2 and shape[0] * shape[1] >= CUT_FROM:
        rows = shape[0] // CUTS
        return [pl.ds(i * rows, rows) for i in range(CUTS)]
    return [slice(None)]


def pieces_of(source, target):
    return [(source.at[part], target.at[part]) for part in cuts(source.shape)]


def first_kernel(tokens, table, gain, wqkv, wproj, *rest):
    nexts, (nw, ne, sw, se), rest = rest[:NEXT], rest[NEXT : NEXT + 4], rest[NEXT + 4 :]
    next_here, (xs, ys, probs, tab, strips, *here, sems, next_sems) = rest[:NEXT], rest[NEXT:]
    next_pairs = [pair for a, b in zip(nexts, next_here) for pair in pieces_of(a, b)]
    next_copies = [pltpu.make_async_copy(a, b, next_sems.at[i]) for i, (a, b) in enumerate(next_pairs)]
    pairs = [pair for a, b in zip((table, tokens, gain, wqkv, wproj), here) for pair in pieces_of(a, b)]
    copies = [pltpu.make_async_copy(a, b, sems.at[i]) for i, (a, b) in enumerate(pairs)]
    for copy in copies:
        copy.start()
    xs[:, WW:, :] = jnp.zeros((WH, PITCH - WW, xs.shape[-1]), F32)
    copies[0].wait()
    bias_strips(here[0], tab, strips)
    copies[1].wait()
    xs[:, :WW, :] = here[1][0].astype(F32)
    copies[2].wait()

    def weights(i):
        for copy in (copies[3:-1], copies[-1:])[i]:
            copy.wait()
        if i == 0:
            for copy in next_copies:
                copy.start()
        return here[3 + i]

    attend(xs, ys, here[2], weights, functools.partial(bias_tiles, strips), probs, None)
    quadrants(ys, (nw, ne, sw, se))
    for copy in next_copies:
        copy.wait()


def bias_kernel(table, out, tab, strips):
    bias_strips(table, tab, strips)
    for pair in range(out.shape[0]):
        for t, tiles in enumerate(bias_tiles(strips, 2 * pair)):
            for u, tile in enumerate(tiles):
                out[pair, t, u] = tile


def second_kernel(nw_in, ne_in, sw_in, se_in, bias, gain, wqkv, wproj, nw, ne, sw, se, xs, ys, probs):
    polar = lax.axis_index("lat") == lax.axis_size("lat") - 1
    xs[:, WW:, :] = jnp.zeros((WH, PITCH - WW, xs.shape[-1]), F32)
    at = 0
    pieces = (nw_in, ne_in, sw_in, se_in)
    for r in (0, HALF_R):
        for c in (0, HALF_C):
            xs[r : r + HALF_R, c : c + HALF_C, :] = pieces[at][...].astype(F32)
            at += 1

    def tiles_of(h):
        return [[bias[h // 2, t, u] for u in range(bias.shape[2])] for t in range(bias.shape[1])]

    attend(xs, ys, gain, lambda i: (wqkv, wproj)[i], tiles_of, probs, polar)
    quadrants(ys, (nw, ne, sw, se))


VMEM = pl.BlockSpec(memory_space=pltpu.VMEM)
HBM = pl.BlockSpec(memory_space=pltpu.HBM)


def bias_room(table):
    _, heads, count = table.shape
    lanes = -(-count // LANES) * LANES
    return [pltpu.VMEM((heads, lanes), F32), pltpu.VMEM((heads, 2, SUB, 3 * LANES), F32)]


def expand(table):
    heads = table.shape[1]
    lane_tiles = 2 * WH * PITCH // LANES
    shape = (heads // 2, lane_tiles, WH * WW // SUB, SUB, LANES)
    return pl.pallas_call(
        bias_kernel,
        out_shape=jax.ShapeDtypeStruct(shape, F32),
        in_specs=[VMEM],
        out_specs=VMEM,
        scratch_shapes=bias_room(table),
        compiler_params=pltpu.CompilerParams(vmem_limit_bytes=8 << 20),
        cost_estimate=pl.CostEstimate(flops=2_000_000, bytes_accessed=1_800_000, transcendentals=0),
    )(table)


def copies_of(arrays):
    return pltpu.SemaphoreType.DMA((sum(len(cuts(a.shape)) for a in arrays),))


def block(kernel, pieces, bias, gain, wqkv, wproj, fetch=()):
    width = wproj.shape[0]
    group = LANES * HEADS // width
    piece = jax.ShapeDtypeStruct((HALF_R, HALF_C, width), BF16)
    args = (*pieces, bias, gain.reshape(1, width), wqkv, wproj)
    scratch = [
        pltpu.VMEM((WH, PITCH, width), F32),
        pltpu.VMEM((WH, PITCH, width), F32),
        pltpu.VMEM((HEADS // group, WH * WW, group * WH * PITCH), BF16),
    ]
    if fetch:
        order = (args[1], args[0], *args[2:])
        scratch += bias_room(bias)
        scratch += [pltpu.VMEM(a.shape, a.dtype) for a in order]
        scratch += [copies_of(order), copies_of(fetch)]
        args = tuple(pltpu.with_memory_space_constraint(a, pltpu.HBM) for a in (*args, *fetch))
    source = HBM if fetch else VMEM
    return pl.pallas_call(
        kernel,
        out_shape=(piece,) * 4 + tuple(jax.ShapeDtypeStruct(a.shape, a.dtype) for a in fetch),
        in_specs=[source] * len(args),
        out_specs=(VMEM,) * (4 + len(fetch)),
        scratch_shapes=scratch,
        compiler_params=pltpu.CompilerParams(vmem_limit_bytes=24 << 20),
        cost_estimate=pl.CostEstimate(flops=400_000_000, bytes_accessed=2_500_000, transcendentals=600_000),
    )(*args)


def moved(piece, lat, lon):
    rows, cols = lax.axis_size("lat"), lax.axis_size("lon")
    route = [
        (((i + lat) % rows) * cols + (j + lon) % cols, i * cols + j) for i in range(rows) for j in range(cols)
    ]
    return lax.ppermute(piece, ("lat", "lon"), route)


def shards(
    tokens,
    gain_first,
    qkv_first,
    proj_first,
    bias_first,
    gain_second,
    qkv_second,
    proj_second,
    bias_second,
):
    nw, ne, sw, se, qkv_second, proj_second = block(
        first_kernel, (tokens,), bias_first, gain_first, qkv_first, proj_first, (qkv_second, proj_second)
    )
    bias = expand(bias_second)
    window = (se, moved(sw, 0, 1), moved(ne, 1, 0), moved(nw, 1, 1))
    nw, ne, sw, se = block(second_kernel, window, bias, gain_second, qkv_second, proj_second)
    west, north, corner = moved(ne, 0, -1), moved(sw, -1, 0), moved(se, -1, -1)
    upper = jnp.concatenate([corner, north], axis=1)
    lower = jnp.concatenate([west, nw], axis=1)
    return jnp.concatenate([upper, lower], axis=0)[None]


def solution(mesh):
    placed = (
        P(None, "lat", "lon", None),
        P(),
        P(),
        P(),
        P("lat", None, None),
        P(),
        P(),
        P(),
        P("lat", None, None),
    )
    return jax.shard_map(
        shards, mesh=mesh, in_specs=placed, out_specs=P(None, "lat", "lon", None), check_vma=False
    )
```

```python
import functools
import math

import jax
import jax.numpy as jnp
from jax import lax
from jax.experimental import pallas as pl
from jax.experimental.pallas import tpu as pltpu
from jax.sharding import PartitionSpec as P


HEADS = 16
CUTS = 4
CUT_FROM = 1 << 19
WH = 12
WW = 12
LANES = 128
SUB = 8
PITCH = 16
SPAN_C = 2 * WW - 1
HALF_R = WH // 2
HALF_C = WW // 2
REST = WW - SUB
NEG = -1e30
LOG2E = math.log2(math.e)
F32 = jnp.float32
BF16 = jnp.bfloat16


def iota(shape, dim):
    return lax.broadcasted_iota(jnp.int32, shape, dim)


def bias_strips(table, tab, strips):
    heads = table.shape[1]
    count = table.shape[2]
    tab[...] = jnp.zeros_like(tab)
    tab[:, :count] = table[0]
    lane = iota((SUB, LANES), 1)
    row = iota((SUB, LANES), 0)
    plans = []
    for tile in range(2):
        for k in range(3):
            u = lane + k * LANES
            step = u // PITCH
            if tile == 0:
                col = row
            else:
                second = row >= REST
                col = SUB + jnp.where(second, row - REST, row)
                step = jnp.where(second, step - 1, step)
            index = step * SPAN_C + u % PITCH - col + WW - 1
            index = jnp.clip(index, 0, count - 1)
            low = max(8 * k - tile, 0) * SPAN_C
            top = min((8 * k + 7) * SPAN_C + PITCH + WW - 2, count - 1)
            sources = range(low // LANES, top // LANES + 1)
            plans.append((tile, k, index % LANES, index // LANES, sources))
    for tile, k, inner, outer, sources in plans:
        values = [None] * heads
        for s in sources:
            here = outer == s
            for h in range(heads):
                row = jnp.broadcast_to(tab[h : h + 1, s * LANES : (s + 1) * LANES], (SUB, LANES))
                taken = jnp.take_along_axis(row, inner, axis=1)
                values[h] = taken if values[h] is None else jnp.where(here, taken, values[h])
        for h in range(heads):
            strips[h, tile, :, k * LANES : (k + 1) * LANES] = values[h] * LOG2E


def bias_tiles(strips, h):
    turned = {}
    lane = iota((SUB, LANES), 1)
    per_head = WH * PITCH

    def turn(head, tile, k, by):
        key = (head, tile, k, by)
        if key not in turned:
            part = strips[head, tile, :, k * LANES : (k + 1) * LANES]
            turned[key] = pltpu.roll(part, LANES - by, 1) if by else part
        return turned[key]

    def window(tile, start, t):
        cuts = []
        at = t * LANES
        while at < (t + 1) * LANES:
            which, query = divmod(at, per_head)
            u = start + query
            k = u // LANES
            end = min(at + (k + 1) * LANES - u, (which + 1) * per_head, (t + 1) * LANES)
            cuts.append((end - t * LANES, turn(h + which, tile, k, (u - at) % LANES)))
            at = end
        value = cuts[-1][1]
        for end, part in reversed(cuts[:-1]):
            value = jnp.where(lane < end, part, value)
        return value

    starts = [(0, PITCH * (WH - 1 - r)) for r in range(WH)]
    starts += [(1, PITCH * (WH - 1 - r)) for r in range(0, WH, 2)]
    return [[window(tile, start, t) for tile, start in starts] for t in range(2 * per_head // LANES)]


def halves(polar):
    lane = iota((SUB, LANES), 1)
    out = []
    for t in range(2 * WH * PITCH // LANES):
        query = (lane + t * LANES) % (WH * PITCH) // PITCH >= HALF_R
        out.append([jnp.where((query != lower) & polar, NEG, 0.0).astype(F32) for lower in (False, True)])
    return out


def compact(value):
    width = value.shape[-1]
    tiles = value.reshape(WH, 2, SUB, width)
    row = iota((SUB, width), 0)
    parts = [tiles[r, 0] for r in range(WH)]
    for r in range(0, WH, 2):
        parts.append(jnp.where(row < REST, tiles[r, 1], pltpu.roll(tiles[r + 1, 1], REST, 0)))
    return jnp.concatenate(parts, axis=0)


def split(value):
    high = value.astype(BF16)
    return high, (value - high.astype(F32)).astype(BF16)


def soft(scores, bias, mask, probs, at):
    count = len(bias)
    tiles = []
    for u in range(count):
        s = scores[u * SUB : (u + 1) * SUB] + bias[u]
        if mask is not None:
            lower = u >= HALF_R if u < WH else 2 * (u - WH) >= HALF_R
            s = s + mask[int(lower)]
        tiles.append(s)
    top = functools.reduce(jnp.maximum, tiles)
    top = jnp.max(top, axis=0, keepdims=True)
    tiles = [jnp.exp2(s - top) for s in tiles]
    total = functools.reduce(jnp.add, tiles)
    inverse = 1.0 / jnp.sum(total, axis=0, keepdims=True)
    for u in range(0, count, 2):
        pair = jnp.concatenate([tiles[u] * inverse, tiles[u + 1] * inverse], axis=0)
        probs[u * SUB : (u + 2) * SUB, at : at + LANES] = pair.astype(BF16)


def attend(xs, ys, gain, weights, tiles_of, probs, polar):
    width = xs.shape[-1]
    head_dim = width // HEADS
    group = LANES // head_dim
    per_head = WH * PITCH
    x = xs[...].reshape(per_head, width)
    mean = jnp.mean(x, axis=-1, keepdims=True)
    centred = x - mean
    var = jnp.mean(centred * centred, axis=-1, keepdims=True)
    normed = (centred * lax.rsqrt(var + 1e-05) * gain[...]).astype(BF16)
    wqkv = weights(0)
    mixed = jnp.dot(normed, wqkv[...], preferred_element_type=F32)
    q_hi, q_lo = split(mixed[:, :width] * (head_dim ** (-0.5) * LOG2E))
    k_hi, k_lo = split(compact(mixed[:, width : 2 * width]))
    values = compact(mixed[:, 2 * width :]).astype(BF16)
    lane = iota((1, LANES), 1)
    masks = None if polar is None else halves(polar)

    def product(g):
        part = slice(g * LANES, (g + 1) * LANES)
        left = jnp.concatenate([k_hi[:, part], k_hi[:, part], k_lo[:, part]], axis=1)
        rights = []
        for i in range(group):
            own = (lane // head_dim == i).astype(BF16)
            high = q_hi[:, part] * own
            rights.append(jnp.concatenate([high, q_lo[:, part] * own, high], axis=1))
        right = jnp.concatenate(rights, axis=0)
        return lax.dot_general(left, right, (((1,), (1,)), ((), ())), preferred_element_type=F32)

    def gather(g):
        part = slice(g * LANES, (g + 1) * LANES)
        mixed_v = lax.dot_general(
            values[:, part], probs[g], (((0,), (0,)), ((), ())), preferred_element_type=F32
        )
        heads_out = []
        for i in range(group):
            rows = slice(i * head_dim, (i + 1) * head_dim)
            first, by = divmod(i * per_head, LANES)
            own = mixed_v[rows, first * LANES : (first + 2) * LANES]
            heads_out.append(pltpu.roll(own, 2 * LANES - by, 1) if by else own)
        return jnp.concatenate(heads_out, axis=0).T

    outs = []
    groups = HEADS // group
    ahead = product(0)
    for g in range(groups):
        scores = ahead
        if g + 1 < groups:
            ahead = product(g + 1)
        if g:
            outs.append(gather(g - 1))
        for i in range(0, group, 2):
            tiles = tiles_of(g * group + i)
            for t in range(len(tiles)):
                at = i * per_head + t * LANES
                soft(scores[:, at : at + LANES], tiles[t], masks and masks[t], probs.at[g], at)
    outs.append(gather(groups - 1))
    heads_out = jnp.concatenate(outs, axis=1)[:per_head].astype(BF16)
    wproj = weights(1)
    branch = jnp.dot(heads_out, wproj[...], preferred_element_type=F32)
    ys[...] = xs[...] + branch.reshape(xs.shape)


CORNERS = [(r, c) for r in (0, HALF_R) for c in (0, HALF_C)]


def quadrants(ys, outs):
    for at, (r, c) in enumerate(CORNERS):
        outs[at][...] = ys[r : r + HALF_R, c : c + HALF_C, :].astype(BF16)


def packed(ys, zs, outs):
    for at, (r, c) in enumerate(CORNERS):
        for i in range(HALF_R):
            zs[at, i * HALF_C : (i + 1) * HALF_C, :] = ys[r + i, c : c + HALF_C, :]
        outs[at][...] = zs[at].astype(BF16)


def unpacked(pieces, zs, xs):
    for at, (r, c) in enumerate(CORNERS):
        zs[at] = pieces[at][...].astype(F32)
        for i in range(HALF_R):
            xs[r + i, c : c + HALF_C, :] = zs[at, i * HALF_C : (i + 1) * HALF_C, :]


def cuts(shape):
    if len(shape) == 2 and shape[0] * shape[1] >= CUT_FROM:
        rows = shape[0] // CUTS
        return [pl.ds(i * rows, rows) for i in range(CUTS)]
    return [slice(None)]


def pieces_of(source, target):
    return [(source.at[part], target.at[part]) for part in cuts(source.shape)]


def first_kernel(tokens, table, gain, wqkv, wproj, nw, ne, sw, se, xs, ys, zs, probs, tab, strips, *here):
    here, sems = here[:-1], here[-1]
    pairs = [pair for a, b in zip((table, tokens, gain, wqkv, wproj), here) for pair in pieces_of(a, b)]
    copies = [pltpu.make_async_copy(a, b, sems.at[i]) for i, (a, b) in enumerate(pairs)]
    for copy in copies:
        copy.start()
    xs[:, WW:, :] = jnp.zeros((WH, PITCH - WW, xs.shape[-1]), F32)
    copies[0].wait()
    bias_strips(here[0], tab, strips)
    copies[1].wait()
    xs[:, :WW, :] = here[1][0].astype(F32)
    copies[2].wait()

    def weights(i):
        for copy in (copies[3:-1], copies[-1:])[i]:
            copy.wait()
        return here[3 + i]

    attend(xs, ys, here[2], weights, functools.partial(bias_tiles, strips), probs, None)
    packed(ys, zs, (nw, ne, sw, se))


def bias_kernel(table, out, tab, strips):
    bias_strips(table, tab, strips)
    for pair in range(out.shape[0]):
        for t, tiles in enumerate(bias_tiles(strips, 2 * pair)):
            for u, tile in enumerate(tiles):
                out[pair, t, u] = tile


def second_kernel(nw_in, ne_in, sw_in, se_in, bias, gain, wqkv, wproj, nw, ne, sw, se, xs, ys, zs, probs):
    polar = lax.axis_index("lat") == lax.axis_size("lat") - 1
    xs[:, WW:, :] = jnp.zeros((WH, PITCH - WW, xs.shape[-1]), F32)
    unpacked((nw_in, ne_in, sw_in, se_in), zs, xs)

    def tiles_of(h):
        return [[bias[h // 2, t, u] for u in range(bias.shape[2])] for t in range(bias.shape[1])]

    attend(xs, ys, gain, lambda i: (wqkv, wproj)[i], tiles_of, probs, polar)
    quadrants(ys, (nw, ne, sw, se))


VMEM = pl.BlockSpec(memory_space=pltpu.VMEM)
HBM = pl.BlockSpec(memory_space=pltpu.HBM)


def bias_room(table):
    _, heads, count = table.shape
    lanes = -(-count // LANES) * LANES
    return [pltpu.VMEM((heads, lanes), F32), pltpu.VMEM((heads, 2, SUB, 3 * LANES), F32)]


def expand(table):
    heads = table.shape[1]
    lane_tiles = 2 * WH * PITCH // LANES
    shape = (heads // 2, lane_tiles, WH * WW // SUB, SUB, LANES)
    return pl.pallas_call(
        bias_kernel,
        out_shape=jax.ShapeDtypeStruct(shape, F32),
        in_specs=[VMEM],
        out_specs=VMEM,
        scratch_shapes=bias_room(table),
        compiler_params=pltpu.CompilerParams(vmem_limit_bytes=8 << 20),
        cost_estimate=pl.CostEstimate(flops=2_000_000, bytes_accessed=1_800_000, transcendentals=0),
    )(table)


def block(kernel, pieces, bias, gain, wqkv, wproj, fetch, shape):
    width = wproj.shape[0]
    group = LANES * HEADS // width
    piece = jax.ShapeDtypeStruct(shape, BF16)
    args = (*pieces, bias, gain.reshape(1, width), wqkv, wproj)
    scratch = [
        pltpu.VMEM((WH, PITCH, width), F32),
        pltpu.VMEM((WH, PITCH, width), F32),
        pltpu.VMEM((4, HALF_R * HALF_C, width), F32),
        pltpu.VMEM((HEADS // group, WH * WW, group * WH * PITCH), BF16),
    ]
    if fetch:
        order = (args[1], args[0], *args[2:])
        scratch += bias_room(bias)
        scratch += [pltpu.VMEM(a.shape, a.dtype) for a in order]
        scratch += [pltpu.SemaphoreType.DMA((sum(len(cuts(a.shape)) for a in order),))]
        args = tuple(pltpu.with_memory_space_constraint(a, pltpu.HBM) for a in args)
    source = HBM if fetch else VMEM
    return pl.pallas_call(
        kernel,
        out_shape=(piece,) * 4,
        in_specs=[source] * len(args),
        out_specs=(VMEM,) * 4,
        scratch_shapes=scratch,
        compiler_params=pltpu.CompilerParams(vmem_limit_bytes=24 << 20),
        cost_estimate=pl.CostEstimate(flops=400_000_000, bytes_accessed=2_500_000, transcendentals=600_000),
    )(*args)


def moved(piece, lat, lon):
    rows, cols = lax.axis_size("lat"), lax.axis_size("lon")
    route = [
        (((i + lat) % rows) * cols + (j + lon) % cols, i * cols + j) for i in range(rows) for j in range(cols)
    ]
    return lax.ppermute(piece, ("lat", "lon"), route)


def shards(
    tokens,
    gain_first,
    qkv_first,
    proj_first,
    bias_first,
    gain_second,
    qkv_second,
    proj_second,
    bias_second,
):
    size = (HALF_R * HALF_C, tokens.shape[-1])
    nw, ne, sw, se = block(
        first_kernel, (tokens,), bias_first, gain_first, qkv_first, proj_first, True, size
    )
    bias = expand(bias_second)
    window = (se, moved(sw, 0, 1), moved(ne, 1, 0), moved(nw, 1, 1))
    size = (HALF_R, HALF_C, tokens.shape[-1])
    nw, ne, sw, se = block(second_kernel, window, bias, gain_second, qkv_second, proj_second, False, size)
    west, north, corner = moved(ne, 0, -1), moved(sw, -1, 0), moved(se, -1, -1)
    upper = jnp.concatenate([corner, north], axis=1)
    lower = jnp.concatenate([west, nw], axis=1)
    return jnp.concatenate([upper, lower], axis=0)[None]


def solution(mesh):
    placed = (
        P(None, "lat", "lon", None),
        P(),
        P(),
        P(),
        P("lat", None, None),
        P(),
        P(),
        P(),
        P("lat", None, None),
    )
    return jax.shard_map(
        shards, mesh=mesh, in_specs=placed, out_specs=P(None, "lat", "lon", None), check_vma=False
    )
```

```python
import functools
import math

import jax
import jax.numpy as jnp
from jax import lax
from jax.experimental import pallas as pl
from jax.experimental.pallas import tpu as pltpu
from jax.sharding import PartitionSpec as P


HEADS = 16
CUTS = 4
CUT_FROM = 1 << 19
WH = 12
WW = 12
LANES = 128
SUB = 8
PITCH = 16
SPAN_C = 2 * WW - 1
HALF_R = WH // 2
HALF_C = WW // 2
REST = WW - SUB
NEG = -1e30
LOG2E = math.log2(math.e)
F32 = jnp.float32
BF16 = jnp.bfloat16


def iota(shape, dim):
    return lax.broadcasted_iota(jnp.int32, shape, dim)


def bias_strips(table, tab, strips):
    heads = table.shape[1]
    count = table.shape[2]
    tab[...] = jnp.zeros_like(tab)
    tab[:, :count] = table[0]
    lane = iota((SUB, LANES), 1)
    row = iota((SUB, LANES), 0)
    plans = []
    for tile in range(2):
        for k in range(3):
            u = lane + k * LANES
            step = u // PITCH
            if tile == 0:
                col = row
            else:
                second = row >= REST
                col = SUB + jnp.where(second, row - REST, row)
                step = jnp.where(second, step - 1, step)
            index = step * SPAN_C + u % PITCH - col + WW - 1
            index = jnp.clip(index, 0, count - 1)
            low = max(8 * k - tile, 0) * SPAN_C
            top = min((8 * k + 7) * SPAN_C + PITCH + WW - 2, count - 1)
            sources = range(low // LANES, top // LANES + 1)
            plans.append((tile, k, index % LANES, index // LANES, sources))
    for tile, k, inner, outer, sources in plans:
        values = [None] * heads
        for s in sources:
            here = outer == s
            for h in range(heads):
                row = jnp.broadcast_to(tab[h : h + 1, s * LANES : (s + 1) * LANES], (SUB, LANES))
                taken = jnp.take_along_axis(row, inner, axis=1)
                values[h] = taken if values[h] is None else jnp.where(here, taken, values[h])
        for h in range(heads):
            strips[h, tile, :, k * LANES : (k + 1) * LANES] = values[h] * LOG2E


def bias_tiles(strips, h):
    turned = {}
    lane = iota((SUB, LANES), 1)
    per_head = WH * PITCH

    def turn(head, tile, k, by):
        key = (head, tile, k, by)
        if key not in turned:
            part = strips[head, tile, :, k * LANES : (k + 1) * LANES]
            turned[key] = pltpu.roll(part, LANES - by, 1) if by else part
        return turned[key]

    def window(tile, start, t):
        cuts = []
        at = t * LANES
        while at < (t + 1) * LANES:
            which, query = divmod(at, per_head)
            u = start + query
            k = u // LANES
            end = min(at + (k + 1) * LANES - u, (which + 1) * per_head, (t + 1) * LANES)
            cuts.append((end - t * LANES, turn(h + which, tile, k, (u - at) % LANES)))
            at = end
        value = cuts[-1][1]
        for end, part in reversed(cuts[:-1]):
            value = jnp.where(lane < end, part, value)
        return value

    starts = [(0, PITCH * (WH - 1 - r)) for r in range(WH)]
    starts += [(1, PITCH * (WH - 1 - r)) for r in range(0, WH, 2)]
    return [[window(tile, start, t) for tile, start in starts] for t in range(2 * per_head // LANES)]


def halves(polar):
    lane = iota((SUB, LANES), 1)
    out = []
    for t in range(2 * WH * PITCH // LANES):
        query = (lane + t * LANES) % (WH * PITCH) // PITCH >= HALF_R
        out.append([jnp.where((query != lower) & polar, NEG, 0.0).astype(F32) for lower in (False, True)])
    return out


def compact(value):
    width = value.shape[-1]
    tiles = value.reshape(WH, 2, SUB, width)
    row = iota((SUB, width), 0)
    parts = [tiles[r, 0] for r in range(WH)]
    for r in range(0, WH, 2):
        parts.append(jnp.where(row < REST, tiles[r, 1], pltpu.roll(tiles[r + 1, 1], REST, 0)))
    return jnp.concatenate(parts, axis=0)


def spread(value):
    width = value.shape[-1]
    tiles = value.reshape(WH * WW // SUB, SUB, width)
    parts = []
    for r in range(WH):
        rest = tiles[WH + r // 2]
        parts += [tiles[r], pltpu.roll(rest, REST, 0) if r % 2 else rest]
    return jnp.concatenate(parts, axis=0)


def split(value):
    high = value.astype(BF16)
    return high, (value - high.astype(F32)).astype(BF16)


def soft(scores, bias, mask, probs, at):
    count = len(bias)
    tiles = []
    for u in range(count):
        s = scores[u * SUB : (u + 1) * SUB] + bias[u]
        if mask is not None:
            lower = u >= HALF_R if u < WH else 2 * (u - WH) >= HALF_R
            s = s + mask[int(lower)]
        tiles.append(s)
    top = functools.reduce(jnp.maximum, tiles)
    top = jnp.max(top, axis=0, keepdims=True)
    tiles = [jnp.exp2(s - top) for s in tiles]
    total = functools.reduce(jnp.add, tiles)
    inverse = 1.0 / jnp.sum(total, axis=0, keepdims=True)
    for u in range(0, count, 2):
        pair = jnp.concatenate([tiles[u] * inverse, tiles[u + 1] * inverse], axis=0)
        probs[u * SUB : (u + 2) * SUB, at : at + LANES] = pair.astype(BF16)


def attend(xs, ys, gain, weights, tiles_of, probs, polar):
    width = xs.shape[-1]
    head_dim = width // HEADS
    group = LANES // head_dim
    per_head = WH * PITCH
    x = compact(xs[...].reshape(per_head, width))
    mean = jnp.mean(x, axis=-1, keepdims=True)
    centred = x - mean
    var = jnp.mean(centred * centred, axis=-1, keepdims=True)
    normed = centred * lax.rsqrt(var + 1e-05) * gain[...]
    spread_out = spread(normed).astype(BF16)
    normed = normed.astype(BF16)
    wqkv = weights(0)
    query = jnp.dot(spread_out, wqkv[:, :width], preferred_element_type=F32)
    mixed = jnp.dot(normed, wqkv[:, width:], preferred_element_type=F32)
    q_hi, q_lo = split(query * (head_dim ** (-0.5) * LOG2E))
    k_hi, k_lo = split(mixed[:, :width])
    values = mixed[:, width:].astype(BF16)
    lane = iota((1, LANES), 1)
    masks = None if polar is None else halves(polar)

    def product(g):
        part = slice(g * LANES, (g + 1) * LANES)
        left = jnp.concatenate([k_hi[:, part], k_hi[:, part], k_lo[:, part]], axis=1)
        rights = []
        for i in range(group):
            own = (lane // head_dim == i).astype(BF16)
            high = q_hi[:, part] * own
            rights.append(jnp.concatenate([high, q_lo[:, part] * own, high], axis=1))
        right = jnp.concatenate(rights, axis=0)
        return lax.dot_general(left, right, (((1,), (1,)), ((), ())), preferred_element_type=F32)

    def gather(g):
        part = slice(g * LANES, (g + 1) * LANES)
        mixed_v = lax.dot_general(
            values[:, part], probs[g], (((0,), (0,)), ((), ())), preferred_element_type=F32
        )
        heads_out = []
        for i in range(group):
            rows = slice(i * head_dim, (i + 1) * head_dim)
            first, by = divmod(i * per_head, LANES)
            own = mixed_v[rows, first * LANES : (first + 2) * LANES]
            heads_out.append(pltpu.roll(own, 2 * LANES - by, 1) if by else own)
        return jnp.concatenate(heads_out, axis=0).T

    outs = []
    groups = HEADS // group
    ahead = product(0)
    for g in range(groups):
        scores = ahead
        if g + 1 < groups:
            ahead = product(g + 1)
        if g:
            outs.append(gather(g - 1))
        for i in range(0, group, 2):
            tiles = tiles_of(g * group + i)
            for t in range(len(tiles)):
                at = i * per_head + t * LANES
                soft(scores[:, at : at + LANES], tiles[t], masks and masks[t], probs.at[g], at)
    outs.append(gather(groups - 1))
    heads_out = jnp.concatenate(outs, axis=1)[:per_head].astype(BF16)
    wproj = weights(1)
    branch = jnp.dot(heads_out, wproj[...], preferred_element_type=F32)
    ys[...] = xs[...] + branch.reshape(xs.shape)


CORNERS = [(r, c) for r in (0, HALF_R) for c in (0, HALF_C)]


def quadrants(ys, outs):
    for at, (r, c) in enumerate(CORNERS):
        outs[at][...] = ys[r : r + HALF_R, c : c + HALF_C, :].astype(BF16)


def packed(ys, zs, outs):
    for at, (r, c) in enumerate(CORNERS):
        for i in range(HALF_R):
            zs[at, i * HALF_C : (i + 1) * HALF_C, :] = ys[r + i, c : c + HALF_C, :]
        outs[at][...] = zs[at].astype(BF16)


def unpacked(pieces, zs, xs):
    for at, (r, c) in enumerate(CORNERS):
        zs[at] = pieces[at][...].astype(F32)
        for i in range(HALF_R):
            xs[r + i, c : c + HALF_C, :] = zs[at, i * HALF_C : (i + 1) * HALF_C, :]


def cuts(shape):
    if len(shape) == 2 and shape[0] * shape[1] >= CUT_FROM:
        rows = shape[0] // CUTS
        return [pl.ds(i * rows, rows) for i in range(CUTS)]
    return [slice(None)]


def pieces_of(source, target):
    return [(source.at[part], target.at[part]) for part in cuts(source.shape)]


def first_kernel(tokens, table, gain, wqkv, wproj, nw, ne, sw, se, xs, ys, zs, probs, tab, strips, *here):
    here, sems = here[:-1], here[-1]
    pairs = [pair for a, b in zip((table, tokens, gain, wqkv, wproj), here) for pair in pieces_of(a, b)]
    copies = [pltpu.make_async_copy(a, b, sems.at[i]) for i, (a, b) in enumerate(pairs)]
    for copy in copies:
        copy.start()
    xs[:, WW:, :] = jnp.zeros((WH, PITCH - WW, xs.shape[-1]), F32)
    copies[0].wait()
    bias_strips(here[0], tab, strips)
    copies[1].wait()
    xs[:, :WW, :] = here[1][0].astype(F32)
    copies[2].wait()

    def weights(i):
        for copy in (copies[3:-1], copies[-1:])[i]:
            copy.wait()
        return here[3 + i]

    attend(xs, ys, here[2], weights, functools.partial(bias_tiles, strips), probs, None)
    packed(ys, zs, (nw, ne, sw, se))


def bias_kernel(table, out, tab, strips):
    bias_strips(table, tab, strips)
    for pair in range(out.shape[0]):
        for t, tiles in enumerate(bias_tiles(strips, 2 * pair)):
            for u, tile in enumerate(tiles):
                out[pair, t, u] = tile


def second_kernel(nw_in, ne_in, sw_in, se_in, bias, gain, wqkv, wproj, nw, ne, sw, se, xs, ys, zs, probs):
    polar = lax.axis_index("lat") == lax.axis_size("lat") - 1
    xs[:, WW:, :] = jnp.zeros((WH, PITCH - WW, xs.shape[-1]), F32)
    unpacked((nw_in, ne_in, sw_in, se_in), zs, xs)

    def tiles_of(h):
        return [[bias[h // 2, t, u] for u in range(bias.shape[2])] for t in range(bias.shape[1])]

    attend(xs, ys, gain, lambda i: (wqkv, wproj)[i], tiles_of, probs, polar)
    quadrants(ys, (nw, ne, sw, se))


VMEM = pl.BlockSpec(memory_space=pltpu.VMEM)
HBM = pl.BlockSpec(memory_space=pltpu.HBM)


def bias_room(table):
    _, heads, count = table.shape
    lanes = -(-count // LANES) * LANES
    return [pltpu.VMEM((heads, lanes), F32), pltpu.VMEM((heads, 2, SUB, 3 * LANES), F32)]


def expand(table):
    heads = table.shape[1]
    lane_tiles = 2 * WH * PITCH // LANES
    shape = (heads // 2, lane_tiles, WH * WW // SUB, SUB, LANES)
    return pl.pallas_call(
        bias_kernel,
        out_shape=jax.ShapeDtypeStruct(shape, F32),
        in_specs=[VMEM],
        out_specs=VMEM,
        scratch_shapes=bias_room(table),
        compiler_params=pltpu.CompilerParams(vmem_limit_bytes=8 << 20),
        cost_estimate=pl.CostEstimate(flops=2_000_000, bytes_accessed=1_800_000, transcendentals=0),
    )(table)


def block(kernel, pieces, bias, gain, wqkv, wproj, fetch, shape):
    width = wproj.shape[0]
    group = LANES * HEADS // width
    piece = jax.ShapeDtypeStruct(shape, BF16)
    args = (*pieces, bias, gain.reshape(1, width), wqkv, wproj)
    scratch = [
        pltpu.VMEM((WH, PITCH, width), F32),
        pltpu.VMEM((WH, PITCH, width), F32),
        pltpu.VMEM((4, HALF_R * HALF_C, width), F32),
        pltpu.VMEM((HEADS // group, WH * WW, group * WH * PITCH), BF16),
    ]
    if fetch:
        order = (args[1], args[0], *args[2:])
        scratch += bias_room(bias)
        scratch += [pltpu.VMEM(a.shape, a.dtype) for a in order]
        scratch += [pltpu.SemaphoreType.DMA((sum(len(cuts(a.shape)) for a in order),))]
        args = tuple(pltpu.with_memory_space_constraint(a, pltpu.HBM) for a in args)
    source = HBM if fetch else VMEM
    return pl.pallas_call(
        kernel,
        out_shape=(piece,) * 4,
        in_specs=[source] * len(args),
        out_specs=(VMEM,) * 4,
        scratch_shapes=scratch,
        compiler_params=pltpu.CompilerParams(vmem_limit_bytes=24 << 20),
        cost_estimate=pl.CostEstimate(flops=400_000_000, bytes_accessed=2_500_000, transcendentals=600_000),
    )(*args)


def moved(piece, lat, lon):
    rows, cols = lax.axis_size("lat"), lax.axis_size("lon")
    route = [
        (((i + lat) % rows) * cols + (j + lon) % cols, i * cols + j) for i in range(rows) for j in range(cols)
    ]
    return lax.ppermute(piece, ("lat", "lon"), route)


def shards(
    tokens,
    gain_first,
    qkv_first,
    proj_first,
    bias_first,
    gain_second,
    qkv_second,
    proj_second,
    bias_second,
):
    size = (HALF_R * HALF_C, tokens.shape[-1])
    nw, ne, sw, se = block(
        first_kernel, (tokens,), bias_first, gain_first, qkv_first, proj_first, True, size
    )
    bias = expand(bias_second)
    window = (se, moved(sw, 0, 1), moved(ne, 1, 0), moved(nw, 1, 1))
    size = (HALF_R, HALF_C, tokens.shape[-1])
    nw, ne, sw, se = block(second_kernel, window, bias, gain_second, qkv_second, proj_second, False, size)
    west, north, corner = moved(ne, 0, -1), moved(sw, -1, 0), moved(se, -1, -1)
    upper = jnp.concatenate([corner, north], axis=1)
    lower = jnp.concatenate([west, nw], axis=1)
    return jnp.concatenate([upper, lower], axis=0)[None]


def solution(mesh):
    placed = (
        P(None, "lat", "lon", None),
        P(),
        P(),
        P(),
        P("lat", None, None),
        P(),
        P(),
        P(),
        P("lat", None, None),
    )
    return jax.shard_map(
        shards, mesh=mesh, in_specs=placed, out_specs=P(None, "lat", "lon", None), check_vma=False
    )
```

```python
import functools
import math

import jax
import jax.numpy as jnp
from jax import lax
from jax.experimental import pallas as pl
from jax.experimental.pallas import tpu as pltpu
from jax.sharding import PartitionSpec as P


HEADS = 16
WH = 12
WW = 12
LANES = 128
SUB = 8
PITCH = 16
SPAN_C = 2 * WW - 1
HALF_R = WH // 2
HALF_C = WW // 2
REST = WW - SUB
NEG = -1e30
LOG2E = math.log2(math.e)
F32 = jnp.float32
BF16 = jnp.bfloat16


def iota(shape, dim):
    return lax.broadcasted_iota(jnp.int32, shape, dim)


def bias_strips(table, tab, strips):
    heads = table.shape[1]
    count = table.shape[2]
    tab[...] = jnp.zeros_like(tab)
    tab[:, :count] = table[0]
    lane = iota((SUB, LANES), 1)
    row = iota((SUB, LANES), 0)
    plans = []
    for tile in range(2):
        for k in range(3):
            u = lane + k * LANES
            step = u // PITCH
            if tile == 0:
                col = row
            else:
                second = row >= REST
                col = SUB + jnp.where(second, row - REST, row)
                step = jnp.where(second, step - 1, step)
            index = step * SPAN_C + u % PITCH - col + WW - 1
            index = jnp.clip(index, 0, count - 1)
            low = max(8 * k - tile, 0) * SPAN_C
            top = min((8 * k + 7) * SPAN_C + PITCH + WW - 2, count - 1)
            sources = range(low // LANES, top // LANES + 1)
            plans.append((tile, k, index % LANES, index // LANES, sources))
    for tile, k, inner, outer, sources in plans:
        values = [None] * heads
        for s in sources:
            here = outer == s
            for h in range(heads):
                row = jnp.broadcast_to(tab[h : h + 1, s * LANES : (s + 1) * LANES], (SUB, LANES))
                taken = jnp.take_along_axis(row, inner, axis=1)
                values[h] = taken if values[h] is None else jnp.where(here, taken, values[h])
        for h in range(heads):
            strips[h, tile, :, k * LANES : (k + 1) * LANES] = values[h] * LOG2E


def bias_tiles(strips, h):
    turned = {}
    lane = iota((SUB, LANES), 1)
    per_head = WH * PITCH

    def turn(head, tile, k, by):
        key = (head, tile, k, by)
        if key not in turned:
            part = strips[head, tile, :, k * LANES : (k + 1) * LANES]
            turned[key] = pltpu.roll(part, LANES - by, 1) if by else part
        return turned[key]

    def window(tile, start, t):
        cuts = []
        at = t * LANES
        while at < (t + 1) * LANES:
            which, query = divmod(at, per_head)
            u = start + query
            k = u // LANES
            end = min(at + (k + 1) * LANES - u, (which + 1) * per_head, (t + 1) * LANES)
            cuts.append((end - t * LANES, turn(h + which, tile, k, (u - at) % LANES)))
            at = end
        value = cuts[-1][1]
        for end, part in reversed(cuts[:-1]):
            value = jnp.where(lane < end, part, value)
        return value

    starts = [(0, PITCH * (WH - 1 - r)) for r in range(WH)]
    starts += [(1, PITCH * (WH - 1 - r)) for r in range(0, WH, 2)]
    return [[window(tile, start, t) for tile, start in starts] for t in range(2 * per_head // LANES)]


def halves(polar):
    lane = iota((SUB, LANES), 1)
    out = []
    for t in range(2 * WH * PITCH // LANES):
        query = (lane + t * LANES) % (WH * PITCH) // PITCH >= HALF_R
        out.append([jnp.where((query != lower) & polar, NEG, 0.0).astype(F32) for lower in (False, True)])
    return out


def compact(value):
    width = value.shape[-1]
    tiles = value.reshape(WH, 2, SUB, width)
    row = iota((SUB, width), 0)
    parts = [tiles[r, 0] for r in range(WH)]
    for r in range(0, WH, 2):
        parts.append(jnp.where(row < REST, tiles[r, 1], pltpu.roll(tiles[r + 1, 1], REST, 0)))
    return jnp.concatenate(parts, axis=0)


def spread(value):
    width = value.shape[-1]
    tiles = value.reshape(WH * WW // SUB, SUB, width)
    parts = []
    for r in range(WH):
        rest = tiles[WH + r // 2]
        parts += [tiles[r], pltpu.roll(rest, REST, 0) if r % 2 else rest]
    return jnp.concatenate(parts, axis=0)


def split(value):
    high = value.astype(BF16)
    return high, (value - high.astype(F32)).astype(BF16)


def soft(scores, bias, mask, probs, at):
    count = len(bias)
    tiles = []
    for u in range(count):
        s = scores[u * SUB : (u + 1) * SUB] + bias[u]
        if mask is not None:
            lower = u >= HALF_R if u < WH else 2 * (u - WH) >= HALF_R
            s = s + mask[int(lower)]
        tiles.append(s)
    top = functools.reduce(jnp.maximum, tiles)
    top = jnp.max(top, axis=0, keepdims=True)
    tiles = [jnp.exp2(s - top) for s in tiles]
    total = functools.reduce(jnp.add, tiles)
    inverse = 1.0 / jnp.sum(total, axis=0, keepdims=True)
    for u in range(0, count, 2):
        pair = jnp.concatenate([tiles[u] * inverse, tiles[u + 1] * inverse], axis=0)
        probs[u * SUB : (u + 2) * SUB, at : at + LANES] = pair.astype(BF16)


def attend(xs, ys, gain, weights, tiles_of, probs, polar):
    width = xs.shape[-1]
    head_dim = width // HEADS
    group = LANES // head_dim
    per_head = WH * PITCH
    x = compact(xs[...].reshape(per_head, width))
    mean = jnp.mean(x, axis=-1, keepdims=True)
    centred = x - mean
    var = jnp.mean(centred * centred, axis=-1, keepdims=True)
    normed = centred * lax.rsqrt(var + 1e-05) * gain[...]
    spread_out = spread(normed).astype(BF16)
    normed = normed.astype(BF16)
    query = jnp.dot(spread_out, weights(0)[...], preferred_element_type=F32)
    keys = jnp.dot(normed, weights(1)[...], preferred_element_type=F32)
    values = jnp.dot(normed, weights(2)[...], preferred_element_type=F32).astype(BF16)
    q_hi, q_lo = split(query * (head_dim ** (-0.5) * LOG2E))
    k_hi, k_lo = split(keys)
    lane = iota((1, LANES), 1)
    masks = None if polar is None else halves(polar)

    def product(g):
        part = slice(g * LANES, (g + 1) * LANES)
        left = jnp.concatenate([k_hi[:, part], k_hi[:, part], k_lo[:, part]], axis=1)
        rights = []
        for i in range(group):
            own = (lane // head_dim == i).astype(BF16)
            high = q_hi[:, part] * own
            rights.append(jnp.concatenate([high, q_lo[:, part] * own, high], axis=1))
        right = jnp.concatenate(rights, axis=0)
        return lax.dot_general(left, right, (((1,), (1,)), ((), ())), preferred_element_type=F32)

    def gather(g):
        part = slice(g * LANES, (g + 1) * LANES)
        mixed_v = lax.dot_general(
            values[:, part], probs[g], (((0,), (0,)), ((), ())), preferred_element_type=F32
        )
        heads_out = []
        for i in range(group):
            rows = slice(i * head_dim, (i + 1) * head_dim)
            first, by = divmod(i * per_head, LANES)
            own = mixed_v[rows, first * LANES : (first + 2) * LANES]
            heads_out.append(pltpu.roll(own, 2 * LANES - by, 1) if by else own)
        return jnp.concatenate(heads_out, axis=0).T

    outs = []
    groups = HEADS // group
    ahead = product(0)
    for g in range(groups):
        scores = ahead
        if g + 1 < groups:
            ahead = product(g + 1)
        if g:
            outs.append(gather(g - 1))
        for i in range(0, group, 2):
            tiles = tiles_of(g * group + i)
            for t in range(len(tiles)):
                at = i * per_head + t * LANES
                soft(scores[:, at : at + LANES], tiles[t], masks and masks[t], probs.at[g], at)
    outs.append(gather(groups - 1))
    heads_out = jnp.concatenate(outs, axis=1)[:per_head].astype(BF16)
    wproj = weights(3)
    branch = jnp.dot(heads_out, wproj[...], preferred_element_type=F32)
    ys[...] = xs[...] + branch.reshape(xs.shape)


CORNERS = [(r, c) for r in (0, HALF_R) for c in (0, HALF_C)]


def quadrants(ys, outs):
    for at, (r, c) in enumerate(CORNERS):
        outs[at][...] = ys[r : r + HALF_R, c : c + HALF_C, :].astype(BF16)


def packed(ys, zs, outs):
    for at, (r, c) in enumerate(CORNERS):
        for i in range(HALF_R):
            zs[at, i * HALF_C : (i + 1) * HALF_C, :] = ys[r + i, c : c + HALF_C, :]
        outs[at][...] = zs[at].astype(BF16)


def unpacked(pieces, zs, xs):
    for at, (r, c) in enumerate(CORNERS):
        zs[at] = pieces[at][...].astype(F32)
        for i in range(HALF_R):
            xs[r + i, c : c + HALF_C, :] = zs[at, i * HALF_C : (i + 1) * HALF_C, :]


def parts_of(wqkv, wproj):
    width = wproj.shape[0]
    return [wqkv.at[:, i * width : (i + 1) * width] for i in range(3)] + [wproj]


def first_kernel(tokens, table, gain, wqkv, wproj, nw, ne, sw, se, xs, ys, zs, probs, tab, strips, *here):
    here, sems = here[:-1], here[-1]
    sources = (table, tokens, gain, *parts_of(wqkv, wproj))
    targets = (*here[:3], *parts_of(*here[3:]))
    copies = [pltpu.make_async_copy(a, b, sems.at[i]) for i, (a, b) in enumerate(zip(sources, targets))]
    for copy in copies:
        copy.start()
    xs[:, WW:, :] = jnp.zeros((WH, PITCH - WW, xs.shape[-1]), F32)
    copies[0].wait()
    bias_strips(here[0], tab, strips)
    copies[1].wait()
    xs[:, :WW, :] = here[1][0].astype(F32)
    copies[2].wait()

    def weights(i):
        copies[3 + i].wait()
        return targets[3 + i]

    attend(xs, ys, here[2], weights, functools.partial(bias_tiles, strips), probs, None)
    packed(ys, zs, (nw, ne, sw, se))


def bias_kernel(table, out, tab, strips):
    bias_strips(table, tab, strips)
    for pair in range(out.shape[0]):
        for t, tiles in enumerate(bias_tiles(strips, 2 * pair)):
            for u, tile in enumerate(tiles):
                out[pair, t, u] = tile


def second_kernel(nw_in, ne_in, sw_in, se_in, bias, gain, wqkv, wproj, nw, ne, sw, se, xs, ys, zs, probs):
    polar = lax.axis_index("lat") == lax.axis_size("lat") - 1
    xs[:, WW:, :] = jnp.zeros((WH, PITCH - WW, xs.shape[-1]), F32)
    unpacked((nw_in, ne_in, sw_in, se_in), zs, xs)

    def tiles_of(h):
        return [[bias[h // 2, t, u] for u in range(bias.shape[2])] for t in range(bias.shape[1])]

    attend(xs, ys, gain, lambda i: parts_of(wqkv, wproj)[i], tiles_of, probs, polar)
    quadrants(ys, (nw, ne, sw, se))


VMEM = pl.BlockSpec(memory_space=pltpu.VMEM)
HBM = pl.BlockSpec(memory_space=pltpu.HBM)


def bias_room(table):
    _, heads, count = table.shape
    lanes = -(-count // LANES) * LANES
    return [pltpu.VMEM((heads, lanes), F32), pltpu.VMEM((heads, 2, SUB, 3 * LANES), F32)]


def expand(table):
    heads = table.shape[1]
    lane_tiles = 2 * WH * PITCH // LANES
    shape = (heads // 2, lane_tiles, WH * WW // SUB, SUB, LANES)
    return pl.pallas_call(
        bias_kernel,
        out_shape=jax.ShapeDtypeStruct(shape, F32),
        in_specs=[VMEM],
        out_specs=VMEM,
        scratch_shapes=bias_room(table),
        compiler_params=pltpu.CompilerParams(vmem_limit_bytes=8 << 20),
        cost_estimate=pl.CostEstimate(flops=2_000_000, bytes_accessed=1_800_000, transcendentals=0),
    )(table)


def block(kernel, pieces, bias, gain, wqkv, wproj, fetch, shape):
    width = wproj.shape[0]
    group = LANES * HEADS // width
    piece = jax.ShapeDtypeStruct(shape, BF16)
    args = (*pieces, bias, gain.reshape(1, width), wqkv, wproj)
    scratch = [
        pltpu.VMEM((WH, PITCH, width), F32),
        pltpu.VMEM((WH, PITCH, width), F32),
        pltpu.VMEM((4, HALF_R * HALF_C, width), F32),
        pltpu.VMEM((HEADS // group, WH * WW, group * WH * PITCH), BF16),
    ]
    if fetch:
        order = (args[1], args[0], *args[2:])
        scratch += bias_room(bias)
        scratch += [pltpu.VMEM(a.shape, a.dtype) for a in order]
        scratch += [pltpu.SemaphoreType.DMA((len(order) + 2,))]
        args = tuple(pltpu.with_memory_space_constraint(a, pltpu.HBM) for a in args)
    source = HBM if fetch else VMEM
    return pl.pallas_call(
        kernel,
        out_shape=(piece,) * 4,
        in_specs=[source] * len(args),
        out_specs=(VMEM,) * 4,
        scratch_shapes=scratch,
        compiler_params=pltpu.CompilerParams(vmem_limit_bytes=24 << 20),
        cost_estimate=pl.CostEstimate(flops=400_000_000, bytes_accessed=2_500_000, transcendentals=600_000),
    )(*args)


def moved(piece, lat, lon):
    rows, cols = lax.axis_size("lat"), lax.axis_size("lon")
    route = [
        (((i + lat) % rows) * cols + (j + lon) % cols, i * cols + j) for i in range(rows) for j in range(cols)
    ]
    return lax.ppermute(piece, ("lat", "lon"), route)


def shards(
    tokens,
    gain_first,
    qkv_first,
    proj_first,
    bias_first,
    gain_second,
    qkv_second,
    proj_second,
    bias_second,
):
    size = (HALF_R * HALF_C, tokens.shape[-1])
    nw, ne, sw, se = block(
        first_kernel, (tokens,), bias_first, gain_first, qkv_first, proj_first, True, size
    )
    bias = expand(bias_second)
    window = (se, moved(sw, 0, 1), moved(ne, 1, 0), moved(nw, 1, 1))
    size = (HALF_R, HALF_C, tokens.shape[-1])
    nw, ne, sw, se = block(second_kernel, window, bias, gain_second, qkv_second, proj_second, False, size)
    west, north, corner = moved(ne, 0, -1), moved(sw, -1, 0), moved(se, -1, -1)
    upper = jnp.concatenate([corner, north], axis=1)
    lower = jnp.concatenate([west, nw], axis=1)
    return jnp.concatenate([upper, lower], axis=0)[None]


def solution(mesh):
    placed = (
        P(None, "lat", "lon", None),
        P(),
        P(),
        P(),
        P("lat", None, None),
        P(),
        P(),
        P(),
        P("lat", None, None),
    )
    return jax.shard_map(
        shards, mesh=mesh, in_specs=placed, out_specs=P(None, "lat", "lon", None), check_vma=False
    )
```

```python
import functools
import math

import jax
import jax.numpy as jnp
from jax import lax
from jax.experimental import pallas as pl
from jax.experimental.pallas import tpu as pltpu
from jax.sharding import PartitionSpec as P


HEADS = 16
CUTS = 4
CUT_FROM = 1 << 19
WH = 12
WW = 12
LANES = 128
SUB = 8
PITCH = 16
SPAN_C = 2 * WW - 1
HALF_R = WH // 2
HALF_C = WW // 2
REST = WW - SUB
NEG = -1e30
LOG2E = math.log2(math.e)
F32 = jnp.float32
BF16 = jnp.bfloat16


def iota(shape, dim):
    return lax.broadcasted_iota(jnp.int32, shape, dim)


def bias_strips(table, tab, strips):
    heads = table.shape[1]
    count = table.shape[2]
    tab[...] = jnp.zeros_like(tab)
    tab[:, :count] = table[0]
    lane = iota((SUB, LANES), 1)
    row = iota((SUB, LANES), 0)
    plans = []
    for tile in range(2):
        for k in range(3):
            u = lane + k * LANES
            step = u // PITCH
            if tile == 0:
                col = row
            else:
                second = row >= REST
                col = SUB + jnp.where(second, row - REST, row)
                step = jnp.where(second, step - 1, step)
            index = step * SPAN_C + u % PITCH - col + WW - 1
            index = jnp.clip(index, 0, count - 1)
            low = max(8 * k - tile, 0) * SPAN_C
            top = min((8 * k + 7) * SPAN_C + PITCH + WW - 2, count - 1)
            sources = range(low // LANES, top // LANES + 1)
            plans.append((tile, k, index % LANES, index // LANES, sources))
    for tile, k, inner, outer, sources in plans:
        values = [None] * heads
        for s in sources:
            here = outer == s
            for h in range(heads):
                row = jnp.broadcast_to(tab[h : h + 1, s * LANES : (s + 1) * LANES], (SUB, LANES))
                taken = jnp.take_along_axis(row, inner, axis=1)
                values[h] = taken if values[h] is None else jnp.where(here, taken, values[h])
        for h in range(heads):
            strips[h, tile, :, k * LANES : (k + 1) * LANES] = values[h] * LOG2E


def bias_tiles(strips, h):
    turned = {}
    lane = iota((SUB, LANES), 1)
    per_head = WH * PITCH

    def turn(head, tile, k, by):
        key = (head, tile, k, by)
        if key not in turned:
            part = strips[head, tile, :, k * LANES : (k + 1) * LANES]
            turned[key] = pltpu.roll(part, LANES - by, 1) if by else part
        return turned[key]

    def window(tile, start, t):
        cuts = []
        at = t * LANES
        while at < (t + 1) * LANES:
            which, query = divmod(at, per_head)
            u = start + query
            k = u // LANES
            end = min(at + (k + 1) * LANES - u, (which + 1) * per_head, (t + 1) * LANES)
            cuts.append((end - t * LANES, turn(h + which, tile, k, (u - at) % LANES)))
            at = end
        value = cuts[-1][1]
        for end, part in reversed(cuts[:-1]):
            value = jnp.where(lane < end, part, value)
        return value

    starts = [(0, PITCH * (WH - 1 - r)) for r in range(WH)]
    starts += [(1, PITCH * (WH - 1 - r)) for r in range(0, WH, 2)]
    return [[window(tile, start, t) for tile, start in starts] for t in range(2 * per_head // LANES)]


def halves(polar):
    lane = iota((SUB, LANES), 1)
    out = []
    for t in range(2 * WH * PITCH // LANES):
        query = (lane + t * LANES) % (WH * PITCH) // PITCH >= HALF_R
        out.append([jnp.where((query != lower) & polar, NEG, 0.0).astype(F32) for lower in (False, True)])
    return out


def compact(value):
    width = value.shape[-1]
    tiles = value.reshape(WH, 2, SUB, width)
    row = iota((SUB, width), 0)
    parts = [tiles[r, 0] for r in range(WH)]
    for r in range(0, WH, 2):
        parts.append(jnp.where(row < REST, tiles[r, 1], pltpu.roll(tiles[r + 1, 1], REST, 0)))
    return jnp.concatenate(parts, axis=0)


def spread(value):
    width = value.shape[-1]
    tiles = value.reshape(WH * WW // SUB, SUB, width)
    parts = []
    for r in range(WH):
        rest = tiles[WH + r // 2]
        parts += [tiles[r], pltpu.roll(rest, REST, 0) if r % 2 else rest]
    return jnp.concatenate(parts, axis=0)


def split(value):
    high = value.astype(BF16)
    return high, (value - high.astype(F32)).astype(BF16)


def soft(scores, bias, probs, at):
    count = len(bias)
    tiles = [scores[u * SUB : (u + 1) * SUB] + bias[u] for u in range(count)]
    top = functools.reduce(jnp.maximum, tiles)
    top = jnp.max(top, axis=0, keepdims=True)
    tiles = [jnp.exp2(s - top) for s in tiles]
    total = functools.reduce(jnp.add, tiles)
    inverse = 1.0 / jnp.sum(total, axis=0, keepdims=True)
    for u in range(0, count, 2):
        pair = jnp.concatenate([tiles[u] * inverse, tiles[u + 1] * inverse], axis=0)
        probs[u * SUB : (u + 2) * SUB, at : at + LANES] = pair.astype(BF16)


def attend(xs, ys, gain, weights, tiles_of, probs):
    width = xs.shape[-1]
    head_dim = width // HEADS
    group = LANES // head_dim
    per_head = WH * PITCH
    x = compact(xs[...].reshape(per_head, width))
    mean = jnp.mean(x, axis=-1, keepdims=True)
    centred = x - mean
    var = jnp.mean(centred * centred, axis=-1, keepdims=True)
    normed = centred * lax.rsqrt(var + 1e-05) * gain[...]
    spread_out = spread(normed).astype(BF16)
    normed = normed.astype(BF16)
    wqkv = weights(0)
    query = jnp.dot(spread_out, wqkv[:, :width], preferred_element_type=F32)
    mixed = jnp.dot(normed, wqkv[:, width:], preferred_element_type=F32)
    q_hi, q_lo = split(query * (head_dim ** (-0.5) * LOG2E))
    k_hi, k_lo = split(mixed[:, :width])
    values = mixed[:, width:].astype(BF16)
    lane = iota((1, LANES), 1)

    def product(g):
        part = slice(g * LANES, (g + 1) * LANES)
        left = jnp.concatenate([k_hi[:, part], k_hi[:, part], k_lo[:, part]], axis=1)
        rights = []
        for i in range(group):
            own = (lane // head_dim == i).astype(BF16)
            high = q_hi[:, part] * own
            rights.append(jnp.concatenate([high, q_lo[:, part] * own, high], axis=1))
        right = jnp.concatenate(rights, axis=0)
        return lax.dot_general(left, right, (((1,), (1,)), ((), ())), preferred_element_type=F32)

    def gather(g):
        part = slice(g * LANES, (g + 1) * LANES)
        turned = values[:, part].T
        heads_out = []
        for i in range(0, group, 2):
            mixed_v = jnp.dot(
                turned[i * head_dim : (i + 2) * head_dim],
                probs[g, :, i * per_head : (i + 2) * per_head],
                preferred_element_type=F32,
            )
            heads_out.append(mixed_v[:head_dim, : 2 * LANES])
            heads_out.append(pltpu.roll(mixed_v[head_dim:, LANES:], 2 * LANES - per_head % LANES, 1))
        return jnp.concatenate(heads_out, axis=0).astype(BF16).T

    outs = []
    groups = HEADS // group
    ahead = product(0)
    for g in range(groups):
        scores = ahead
        if g + 1 < groups:
            ahead = product(g + 1)
        if g:
            outs.append(gather(g - 1))
        for i in range(0, group, 2):
            tiles = tiles_of(g * group + i)
            for t in range(len(tiles)):
                at = i * per_head + t * LANES
                soft(scores[:, at : at + LANES], tiles[t], probs.at[g], at)
    outs.append(gather(groups - 1))
    heads_out = jnp.concatenate(outs, axis=1)[:per_head]
    wproj = weights(1)
    branch = jnp.dot(heads_out, wproj[...], preferred_element_type=F32)
    ys[...] = xs[...] + branch.reshape(xs.shape)


CORNERS = [(r, c) for r in (0, HALF_R) for c in (0, HALF_C)]


def quadrants(ys, outs):
    for at, (r, c) in enumerate(CORNERS):
        outs[at][...] = ys[r : r + HALF_R, c : c + HALF_C, :].astype(BF16)


def packed(ys, zs, outs):
    for at, (r, c) in enumerate(CORNERS):
        for i in range(HALF_R):
            zs[at, i * HALF_C : (i + 1) * HALF_C, :] = ys[r + i, c : c + HALF_C, :]
        outs[at][...] = zs[at].astype(BF16)


def unpacked(pieces, zs, xs):
    for at, (r, c) in enumerate(CORNERS):
        zs[at] = pieces[at][...].astype(F32)
        for i in range(HALF_R):
            xs[r + i, c : c + HALF_C, :] = zs[at, i * HALF_C : (i + 1) * HALF_C, :]


def cuts(shape):
    if len(shape) == 2 and shape[0] * shape[1] >= CUT_FROM:
        rows = shape[0] // CUTS
        return [pl.ds(i * rows, rows) for i in range(CUTS)]
    return [slice(None)]


def pieces_of(source, target):
    return [(source.at[part], target.at[part]) for part in cuts(source.shape)]


def first_kernel(tokens, table, gain, wqkv, wproj, nw, ne, sw, se, xs, ys, zs, probs, tab, strips, *here):
    here, sems = here[:-1], here[-1]
    pairs = [pair for a, b in zip((table, tokens, gain, wqkv, wproj), here) for pair in pieces_of(a, b)]
    copies = [pltpu.make_async_copy(a, b, sems.at[i]) for i, (a, b) in enumerate(pairs)]
    for copy in copies:
        copy.start()
    xs[:, WW:, :] = jnp.zeros((WH, PITCH - WW, xs.shape[-1]), F32)
    copies[0].wait()
    bias_strips(here[0], tab, strips)
    copies[1].wait()
    xs[:, :WW, :] = here[1][0].astype(F32)
    copies[2].wait()

    def weights(i):
        for copy in (copies[3:-1], copies[-1:])[i]:
            copy.wait()
        return here[3 + i]

    attend(xs, ys, here[2], weights, functools.partial(bias_tiles, strips), probs)
    packed(ys, zs, (nw, ne, sw, se))


def bias_kernel(table, out, tab, strips):
    masks = halves(lax.axis_index("lat") == lax.axis_size("lat") - 1)
    bias_strips(table, tab, strips)
    for pair in range(out.shape[0]):
        for t, tiles in enumerate(bias_tiles(strips, 2 * pair)):
            for u, tile in enumerate(tiles):
                lower = u >= HALF_R if u < WH else 2 * (u - WH) >= HALF_R
                out[pair, t, u] = tile + masks[t][int(lower)]


def second_kernel(nw_in, ne_in, sw_in, se_in, bias, gain, wqkv, wproj, nw, ne, sw, se, xs, ys, zs, probs):
    xs[:, WW:, :] = jnp.zeros((WH, PITCH - WW, xs.shape[-1]), F32)
    unpacked((nw_in, ne_in, sw_in, se_in), zs, xs)

    def tiles_of(h):
        return [[bias[h // 2, t, u] for u in range(bias.shape[2])] for t in range(bias.shape[1])]

    attend(xs, ys, gain, lambda i: (wqkv, wproj)[i], tiles_of, probs)
    quadrants(ys, (nw, ne, sw, se))


VMEM = pl.BlockSpec(memory_space=pltpu.VMEM)
HBM = pl.BlockSpec(memory_space=pltpu.HBM)


def bias_room(table):
    _, heads, count = table.shape
    lanes = -(-count // LANES) * LANES
    return [pltpu.VMEM((heads, lanes), F32), pltpu.VMEM((heads, 2, SUB, 3 * LANES), F32)]


def expand(table):
    heads = table.shape[1]
    lane_tiles = 2 * WH * PITCH // LANES
    shape = (heads // 2, lane_tiles, WH * WW // SUB, SUB, LANES)
    return pl.pallas_call(
        bias_kernel,
        out_shape=jax.ShapeDtypeStruct(shape, F32),
        in_specs=[VMEM],
        out_specs=VMEM,
        scratch_shapes=bias_room(table),
        compiler_params=pltpu.CompilerParams(vmem_limit_bytes=8 << 20),
        cost_estimate=pl.CostEstimate(flops=2_000_000, bytes_accessed=1_800_000, transcendentals=0),
    )(table)


def block(kernel, pieces, bias, gain, wqkv, wproj, fetch, shape):
    width = wproj.shape[0]
    group = LANES * HEADS // width
    piece = jax.ShapeDtypeStruct(shape, BF16)
    args = (*pieces, bias, gain.reshape(1, width), wqkv, wproj)
    scratch = [
        pltpu.VMEM((WH, PITCH, width), F32),
        pltpu.VMEM((WH, PITCH, width), F32),
        pltpu.VMEM((4, HALF_R * HALF_C, width), F32),
        pltpu.VMEM((HEADS // group, WH * WW, group * WH * PITCH), BF16),
    ]
    if fetch:
        order = (args[1], args[0], *args[2:])
        scratch += bias_room(bias)
        scratch += [pltpu.VMEM(a.shape, a.dtype) for a in order]
        scratch += [pltpu.SemaphoreType.DMA((sum(len(cuts(a.shape)) for a in order),))]
        args = tuple(pltpu.with_memory_space_constraint(a, pltpu.HBM) for a in args)
    source = HBM if fetch else VMEM
    return pl.pallas_call(
        kernel,
        out_shape=(pltpu.VMEM(shape, BF16) if fetch else piece,) * 4,
        in_specs=[source] * len(args),
        out_specs=(VMEM,) * 4,
        scratch_shapes=scratch,
        compiler_params=pltpu.CompilerParams(vmem_limit_bytes=(63 if fetch else 24) << 20),
        cost_estimate=pl.CostEstimate(flops=400_000_000, bytes_accessed=2_500_000, transcendentals=600_000),
    )(*args)


def moved(piece, lat, lon):
    rows, cols = lax.axis_size("lat"), lax.axis_size("lon")
    route = [
        (((i + lat) % rows) * cols + (j + lon) % cols, i * cols + j) for i in range(rows) for j in range(cols)
    ]
    return lax.ppermute(piece, ("lat", "lon"), route)


def shards(
    tokens,
    gain_first,
    qkv_first,
    proj_first,
    bias_first,
    gain_second,
    qkv_second,
    proj_second,
    bias_second,
):
    size = (HALF_R * HALF_C, tokens.shape[-1])
    nw, ne, sw, se = block(
        first_kernel, (tokens,), bias_first, gain_first, qkv_first, proj_first, True, size
    )
    bias = expand(bias_second)
    window = (se, moved(sw, 0, 1), moved(ne, 1, 0), moved(nw, 1, 1))
    size = (HALF_R, HALF_C, tokens.shape[-1])
    nw, ne, sw, se = block(second_kernel, window, bias, gain_second, qkv_second, proj_second, False, size)
    west, north, corner = moved(ne, 0, -1), moved(sw, -1, 0), moved(se, -1, -1)
    upper = jnp.concatenate([corner, north], axis=1)
    lower = jnp.concatenate([west, nw], axis=1)
    return jnp.concatenate([upper, lower], axis=0)[None]


def solution(mesh):
    placed = (
        P(None, "lat", "lon", None),
        P(),
        P(),
        P(),
        P("lat", None, None),
        P(),
        P(),
        P(),
        P("lat", None, None),
    )
    return jax.shard_map(
        shards, mesh=mesh, in_specs=placed, out_specs=P(None, "lat", "lon", None), check_vma=False
    )
```

```python
import functools
import math

import jax
import jax.numpy as jnp
from jax import lax
from jax.experimental import pallas as pl
from jax.experimental.pallas import tpu as pltpu
from jax.sharding import PartitionSpec as P


HEADS = 16
CUTS = 2
CUT_FROM = 1 << 19
WH = 12
WW = 12
LANES = 128
SUB = 8
PITCH = 16
SPAN_C = 2 * WW - 1
HALF_R = WH // 2
HALF_C = WW // 2
REST = WW - SUB
NEG = -1e30
LOG2E = math.log2(math.e)
F32 = jnp.float32
BF16 = jnp.bfloat16


def iota(shape, dim):
    return lax.broadcasted_iota(jnp.int32, shape, dim)


def bias_strips(table, tab, strips):
    heads = table.shape[1]
    count = table.shape[2]
    tab[...] = jnp.zeros_like(tab)
    tab[:, :count] = table[0]
    lane = iota((SUB, LANES), 1)
    row = iota((SUB, LANES), 0)
    plans = []
    for tile in range(2):
        for k in range(3):
            u = lane + k * LANES
            step = u // PITCH
            if tile == 0:
                col = row
            else:
                second = row >= REST
                col = SUB + jnp.where(second, row - REST, row)
                step = jnp.where(second, step - 1, step)
            index = step * SPAN_C + u % PITCH - col + WW - 1
            index = jnp.clip(index, 0, count - 1)
            low = max(8 * k - tile, 0) * SPAN_C
            top = min((8 * k + 7) * SPAN_C + PITCH + WW - 2, count - 1)
            sources = range(low // LANES, top // LANES + 1)
            plans.append((tile, k, index % LANES, index // LANES, sources))
    for tile, k, inner, outer, sources in plans:
        values = [None] * heads
        for s in sources:
            here = outer == s
            for h in range(heads):
                row = jnp.broadcast_to(tab[h : h + 1, s * LANES : (s + 1) * LANES], (SUB, LANES))
                taken = jnp.take_along_axis(row, inner, axis=1)
                values[h] = taken if values[h] is None else jnp.where(here, taken, values[h])
        for h in range(heads):
            strips[h, tile, :, k * LANES : (k + 1) * LANES] = values[h] * LOG2E


def bias_tiles(strips, h):
    turned = {}
    lane = iota((SUB, LANES), 1)
    per_head = WH * PITCH

    def turn(head, tile, k, by):
        key = (head, tile, k, by)
        if key not in turned:
            part = strips[head, tile, :, k * LANES : (k + 1) * LANES]
            turned[key] = pltpu.roll(part, LANES - by, 1) if by else part
        return turned[key]

    def window(tile, start, t):
        cuts = []
        at = t * LANES
        while at < (t + 1) * LANES:
            which, query = divmod(at, per_head)
            u = start + query
            k = u // LANES
            end = min(at + (k + 1) * LANES - u, (which + 1) * per_head, (t + 1) * LANES)
            cuts.append((end - t * LANES, turn(h + which, tile, k, (u - at) % LANES)))
            at = end
        value = cuts[-1][1]
        for end, part in reversed(cuts[:-1]):
            value = jnp.where(lane < end, part, value)
        return value

    starts = [(0, PITCH * (WH - 1 - r)) for r in range(WH)]
    starts += [(1, PITCH * (WH - 1 - r)) for r in range(0, WH, 2)]
    return [[window(tile, start, t) for tile, start in starts] for t in range(2 * per_head // LANES)]


def halves(polar):
    lane = iota((SUB, LANES), 1)
    out = []
    for t in range(2 * WH * PITCH // LANES):
        query = (lane + t * LANES) % (WH * PITCH) // PITCH >= HALF_R
        out.append([jnp.where((query != lower) & polar, NEG, 0.0).astype(F32) for lower in (False, True)])
    return out


def compact(value):
    width = value.shape[-1]
    tiles = value.reshape(WH, 2, SUB, width)
    row = iota((SUB, width), 0)
    parts = [tiles[r, 0] for r in range(WH)]
    for r in range(0, WH, 2):
        parts.append(jnp.where(row < REST, tiles[r, 1], pltpu.roll(tiles[r + 1, 1], REST, 0)))
    return jnp.concatenate(parts, axis=0)


def spread(value):
    width = value.shape[-1]
    tiles = value.reshape(WH * WW // SUB, SUB, width)
    parts = []
    for r in range(WH):
        rest = tiles[WH + r // 2]
        parts += [tiles[r], pltpu.roll(rest, REST, 0) if r % 2 else rest]
    return jnp.concatenate(parts, axis=0)


def split(value):
    high = value.astype(BF16)
    return high, (value - high.astype(F32)).astype(BF16)


def soft(scores, bias, probs, at):
    count = len(bias)
    tiles = [scores[u * SUB : (u + 1) * SUB] + bias[u] for u in range(count)]
    top = functools.reduce(jnp.maximum, tiles)
    top = jnp.max(top, axis=0, keepdims=True)
    tiles = [jnp.exp2(s - top) for s in tiles]
    total = functools.reduce(jnp.add, tiles)
    inverse = 1.0 / jnp.sum(total, axis=0, keepdims=True)
    for u in range(0, count, 2):
        pair = jnp.concatenate([tiles[u] * inverse, tiles[u + 1] * inverse], axis=0)
        probs[u * SUB : (u + 2) * SUB, at : at + LANES] = pair.astype(BF16)


def attend(xs, ys, gain, weights, tiles_of, probs):
    width = xs.shape[-1]
    head_dim = width // HEADS
    group = LANES // head_dim
    per_head = WH * PITCH
    x = compact(xs[...].reshape(per_head, width))
    mean = jnp.mean(x, axis=-1, keepdims=True)
    centred = x - mean
    var = jnp.mean(centred * centred, axis=-1, keepdims=True)
    normed = centred * lax.rsqrt(var + 1e-05) * gain[...]
    spread_out = spread(normed).astype(BF16)
    normed = normed.astype(BF16)
    wqkv = weights(0)
    query = jnp.dot(spread_out, wqkv[:, :width], preferred_element_type=F32)
    mixed = jnp.dot(normed, wqkv[:, width:], preferred_element_type=F32)
    q_hi, q_lo = split(query * (head_dim ** (-0.5) * LOG2E))
    k_hi, k_lo = split(mixed[:, :width])
    values = mixed[:, width:].astype(BF16)
    lane = iota((1, LANES), 1)

    def product(g):
        part = slice(g * LANES, (g + 1) * LANES)
        left = jnp.concatenate([k_hi[:, part], k_hi[:, part], k_lo[:, part]], axis=1)
        rights = []
        for i in range(group):
            own = (lane // head_dim == i).astype(BF16)
            high = q_hi[:, part] * own
            rights.append(jnp.concatenate([high, q_lo[:, part] * own, high], axis=1))
        right = jnp.concatenate(rights, axis=0)
        return lax.dot_general(left, right, (((1,), (1,)), ((), ())), preferred_element_type=F32)

    def gather(g):
        part = slice(g * LANES, (g + 1) * LANES)
        turned = values[:, part].T
        heads_out = []
        for i in range(0, group, 2):
            mixed_v = jnp.dot(
                turned[i * head_dim : (i + 2) * head_dim],
                probs[g, :, i * per_head : (i + 2) * per_head],
                preferred_element_type=F32,
            )
            heads_out.append(mixed_v[:head_dim, : 2 * LANES])
            heads_out.append(pltpu.roll(mixed_v[head_dim:, LANES:], 2 * LANES - per_head % LANES, 1))
        return jnp.concatenate(heads_out, axis=0).astype(BF16).T

    outs = []
    groups = HEADS // group
    ahead = product(0)
    for g in range(groups):
        scores = ahead
        if g + 1 < groups:
            ahead = product(g + 1)
        if g:
            outs.append(gather(g - 1))
        for i in range(0, group, 2):
            tiles = tiles_of(g * group + i)
            for t in range(len(tiles)):
                at = i * per_head + t * LANES
                soft(scores[:, at : at + LANES], tiles[t], probs.at[g], at)
    outs.append(gather(groups - 1))
    heads_out = jnp.concatenate(outs, axis=1)[:per_head]
    wproj = weights(1)
    branch = jnp.dot(heads_out, wproj[...], preferred_element_type=F32)
    ys[...] = xs[...] + branch.reshape(xs.shape)


CORNERS = [(r, c) for r in (0, HALF_R) for c in (0, HALF_C)]


def packed(ys, zs, outs):
    for at, (r, c) in enumerate(CORNERS):
        for i in range(HALF_R):
            zs[at, i * HALF_C : (i + 1) * HALF_C, :] = ys[r + i, c : c + HALF_C, :]
        outs[at][...] = zs[at].astype(BF16)


def unpacked(pieces, zs, xs):
    for at, (r, c) in enumerate(CORNERS):
        zs[at] = pieces[at][...].astype(F32)
        for i in range(HALF_R):
            xs[r + i, c : c + HALF_C, :] = zs[at, i * HALF_C : (i + 1) * HALF_C, :]


def cuts(shape):
    if len(shape) == 2 and shape[0] * shape[1] >= CUT_FROM:
        rows = shape[0] // CUTS
        return [pl.ds(i * rows, rows) for i in range(CUTS)]
    return [slice(None)]


def pieces_of(source, target):
    return [(source.at[part], target.at[part]) for part in cuts(source.shape)]


def first_kernel(tokens, table, gain, wqkv, wproj, nw, ne, sw, se, xs, ys, zs, probs, tab, strips, *here):
    here, sems = here[:-1], here[-1]
    pairs = [pair for a, b in zip((table, tokens, gain, wqkv, wproj), here) for pair in pieces_of(a, b)]
    copies = [pltpu.make_async_copy(a, b, sems.at[i]) for i, (a, b) in enumerate(pairs)]
    for copy in copies:
        copy.start()
    xs[:, WW:, :] = jnp.zeros((WH, PITCH - WW, xs.shape[-1]), F32)
    copies[0].wait()
    bias_strips(here[0], tab, strips)
    copies[1].wait()
    xs[:, :WW, :] = here[1][0].astype(F32)
    copies[2].wait()

    def weights(i):
        for copy in (copies[3:-1], copies[-1:])[i]:
            copy.wait()
        return here[3 + i]

    attend(xs, ys, here[2], weights, functools.partial(bias_tiles, strips), probs)
    packed(ys, zs, (nw, ne, sw, se))


def bias_kernel(table, out, tab, strips):
    masks = halves(lax.axis_index("lat") == lax.axis_size("lat") - 1)
    bias_strips(table, tab, strips)
    for pair in range(out.shape[0]):
        for t, tiles in enumerate(bias_tiles(strips, 2 * pair)):
            for u, tile in enumerate(tiles):
                lower = u >= HALF_R if u < WH else 2 * (u - WH) >= HALF_R
                out[pair, t, u] = tile + masks[t][int(lower)]


def second_kernel(nw_in, ne_in, sw_in, se_in, bias, gain, wqkv, wproj, nw, ne, sw, se, xs, ys, zs, probs):
    xs[:, WW:, :] = jnp.zeros((WH, PITCH - WW, xs.shape[-1]), F32)
    unpacked((nw_in, ne_in, sw_in, se_in), zs, xs)

    def tiles_of(h):
        return [[bias[h // 2, t, u] for u in range(bias.shape[2])] for t in range(bias.shape[1])]

    attend(xs, ys, gain, lambda i: (wqkv, wproj)[i], tiles_of, probs)
    packed(ys, zs, (nw, ne, sw, se))


VMEM = pl.BlockSpec(memory_space=pltpu.VMEM)
HBM = pl.BlockSpec(memory_space=pltpu.HBM)


def bias_room(table):
    _, heads, count = table.shape
    lanes = -(-count // LANES) * LANES
    return [pltpu.VMEM((heads, lanes), F32), pltpu.VMEM((heads, 2, SUB, 3 * LANES), F32)]


def expand(table):
    heads = table.shape[1]
    lane_tiles = 2 * WH * PITCH // LANES
    shape = (heads // 2, lane_tiles, WH * WW // SUB, SUB, LANES)
    return pl.pallas_call(
        bias_kernel,
        out_shape=jax.ShapeDtypeStruct(shape, F32),
        in_specs=[VMEM],
        out_specs=VMEM,
        scratch_shapes=bias_room(table),
        compiler_params=pltpu.CompilerParams(vmem_limit_bytes=8 << 20),
        cost_estimate=pl.CostEstimate(flops=2_000_000, bytes_accessed=1_800_000, transcendentals=0),
    )(table)


def block(kernel, pieces, bias, gain, wqkv, wproj, fetch, shape):
    width = wproj.shape[0]
    group = LANES * HEADS // width
    piece = jax.ShapeDtypeStruct(shape, BF16)
    args = (*pieces, bias, gain.reshape(1, width), wqkv, wproj)
    scratch = [
        pltpu.VMEM((WH, PITCH, width), F32),
        pltpu.VMEM((WH, PITCH, width), F32),
        pltpu.VMEM((4, HALF_R * HALF_C, width), F32),
        pltpu.VMEM((HEADS // group, WH * WW, group * WH * PITCH), BF16),
    ]
    if fetch:
        order = (args[1], args[0], *args[2:])
        scratch += bias_room(bias)
        scratch += [pltpu.VMEM(a.shape, a.dtype) for a in order]
        scratch += [pltpu.SemaphoreType.DMA((sum(len(cuts(a.shape)) for a in order),))]
        args = tuple(pltpu.with_memory_space_constraint(a, pltpu.HBM) for a in args)
    source = HBM if fetch else VMEM
    return pl.pallas_call(
        kernel,
        out_shape=(pltpu.VMEM(shape, BF16) if fetch else piece,) * 4,
        in_specs=[source] * len(args),
        out_specs=(VMEM,) * 4,
        scratch_shapes=scratch,
        compiler_params=pltpu.CompilerParams(vmem_limit_bytes=(63 if fetch else 24) << 20),
        cost_estimate=pl.CostEstimate(flops=400_000_000, bytes_accessed=2_500_000, transcendentals=600_000),
    )(*args)


def join_kernel(nw, ne, sw, se, out, ys, zs):
    unpacked((nw, ne, sw, se), zs, ys)
    out[0] = ys[:, :WW, :].astype(BF16)


def join(*pieces):
    width = pieces[0].shape[-1]
    return pl.pallas_call(
        join_kernel,
        out_shape=jax.ShapeDtypeStruct((1, WH, WW, width), BF16),
        in_specs=[VMEM] * 4,
        out_specs=VMEM,
        scratch_shapes=[
            pltpu.VMEM((WH, PITCH, width), F32),
            pltpu.VMEM((4, HALF_R * HALF_C, width), F32),
        ],
        compiler_params=pltpu.CompilerParams(vmem_limit_bytes=8 << 20),
    )(*pieces)


def moved(piece, lat, lon):
    rows, cols = lax.axis_size("lat"), lax.axis_size("lon")
    route = [
        (((i + lat) % rows) * cols + (j + lon) % cols, i * cols + j) for i in range(rows) for j in range(cols)
    ]
    return lax.ppermute(piece, ("lat", "lon"), route)


def shards(
    tokens,
    gain_first,
    qkv_first,
    proj_first,
    bias_first,
    gain_second,
    qkv_second,
    proj_second,
    bias_second,
):
    size = (HALF_R * HALF_C, tokens.shape[-1])
    nw, ne, sw, se = block(
        first_kernel, (tokens,), bias_first, gain_first, qkv_first, proj_first, True, size
    )
    bias = expand(bias_second)
    window = (se, moved(sw, 0, 1), moved(ne, 1, 0), moved(nw, 1, 1))
    nw, ne, sw, se = block(second_kernel, window, bias, gain_second, qkv_second, proj_second, False, size)
    west, north, corner = moved(ne, 0, -1), moved(sw, -1, 0), moved(se, -1, -1)
    return join(corner, north, west, nw)


def solution(mesh):
    placed = (
        P(None, "lat", "lon", None),
        P(),
        P(),
        P(),
        P("lat", None, None),
        P(),
        P(),
        P(),
        P("lat", None, None),
    )
    return jax.shard_map(
        shards, mesh=mesh, in_specs=placed, out_specs=P(None, "lat", "lon", None), check_vma=False
    )
```
